512 devices in a mesh: group: 16 (over y, core), inner: 32 (over x, z).
Axes of the slice: x: 4, y: 8, z: 8, core: 2. Of those that a mesh axis runs over, the one named last changes fastest.
Arguments:
- pair_rows: bfloat16 [8192, 2048], P(('group', 'inner')), may hold values from -6 to 6
- group_ids: int32 [8192, 1], P(('group', 'inner')), may hold values from 0 to 15; in each aligned block of 16 rows (0 to 15, 16 to 31, ...) at most 2 rows name the same one
- local_ids: int32 [8192, 1], P(('group', 'inner')), may hold values from 0 to 1
- route_weight: float32 [8192], P(('group', 'inner')), may hold values from 0.3 to 1
- w_up: bfloat16 [32, 2048, 8192], P('group', None, 'inner'), may hold values from -0.125 to 0.125
- w_down: bfloat16 [32, 8192, 2048], P('group', 'inner'), may hold values from -0.0625 to 0.0625
Outputs:
- mixed: bfloat16 [8192, 2048], P(('group', 'inner'))
The draws below stay inside these ranges and needn't reach their ends.
Inputs may be any that keep to these rules, and one draw needn't show every extreme that they name: `group_ids`: among the rows of one device no value is named more than 2 times, a bound that some block reaches.
All inputs are finite; a program needn't handle non-finite values.
Results may differ from the reference program's by a relative error of at most 0.02.
Values may be sent and summed in bfloat16 or wider, within the bound.
A program may use at most 64 MiB of HBM per device.

```python
import math
import jax
import jax.numpy as jnp
import numpy as np
from jax import lax

D = 2048
FF = 8192
EXP_GROUP = 2
ROWS_DEV = 16
GCAP = 2
EXPERTS = 32
TOKENS = 8192
N_GROUP = 16
N_INNER = 32


def set_ends(array, key, smallest, largest):
    longest = array.shape.index(max(array.shape))
    spots = []
    for shift in (0, 1):
        where = [jax.random.randint(jax.random.fold_in(key, axis), (), 0, length) for axis, length in enumerate(array.shape)]
        where[longest] = (where[longest] + shift) % array.shape[longest]
        spots.append(tuple(where))
    return array.at[spots[0]].set(smallest).at[spots[1]].set(largest)


def levels(rng, extent, cuts, low, high):
    gain, own = 1.0, jax.random.fold_in(rng, 6)
    for dim, parts in cuts:
        heights = jnp.exp(jax.random.uniform(jax.random.fold_in(own, dim), (parts,), jnp.float32, low / len(cuts), high / len(cuts)))
        gain = gain * jnp.repeat(heights, extent[dim] // parts).reshape([-1 if axis == dim else 1 for axis in range(len(extent))])
    return gain


def shared_out(key, own, number, rows, number_of, top, most, slope):
    order = jax.random.permutation(key, number_of)
    packed, usual = load_shares(number_of, rows * top, most, slope, True), load_shares(number_of, rows * top, most, slope, False)
    places = jnp.arange(number_of)

    def named(tallies, rotation):
        used = int((tallies > 0).sum())
        fixed = max(1, used // 4)
        shifted = fixed + (places - fixed + rotation * (used - fixed)) % max(1, number_of - fixed)
        return jnp.zeros((number_of,), jnp.int32).at[order[jnp.where(places < fixed, places, shifted)]].set(jnp.asarray(tallies, jnp.int32))

    tallies = jnp.where(number % 4 == 0, named(packed, number // 4), named(usual, number - number // 4 - 1))
    mixed = jax.random.permutation(jax.random.fold_in(own, 3), number_of)
    giver, sink = mixed[0:number_of // 2 * 2:2], mixed[1:number_of // 2 * 2:2]
    margin = jnp.minimum(tallies[giver] - 1, most - tallies[sink]) // 2
    margin = jnp.where((giver == order[0]) | (sink == order[0]) | (tallies[sink] == 0), 0, jnp.maximum(margin, 0))
    shifted = jax.random.randint(jax.random.fold_in(own, 4), (number_of // 2,), 0, 1 << 20) % (margin + 1)
    tallies = tallies.at[giver].add(-shifted).at[sink].add(shifted)
    labels = jnp.searchsorted(jnp.cumsum(tallies), jnp.arange(rows * top), side="right").astype(jnp.int32)
    grid = labels.reshape(top, rows).T
    grid = grid[jax.random.permutation(jax.random.fold_in(own, 1), rows)]
    rotation = jax.random.randint(jax.random.fold_in(own, 2), (rows, 1), 0, top)
    return jnp.take_along_axis(grid, (jnp.arange(top)[None, :] + rotation) % top, axis=1)


def load_shares(amount, total, bound, lean, full):
    weights = [(1 << 20) // math.isqrt(standing ** lean) + 1 for standing in range(1, amount + 1)]
    largest = bound if full else min(bound, max(-(-total // amount), total * weights[0] // sum(weights)))
    least = 1 if total - largest >= amount - 1 else 0
    holding, rest = [largest] + [least] * (amount - 1), total - largest - least * (amount - 1)
    while rest > 0:
        candidates = [i for i in range(1, amount) if holding[i] < largest] or [i for i in range(1, amount) if holding[i] < bound]
        whole, remaining = sum([weights[i] for i in candidates]), rest
        for i in candidates:
            addition = min(bound - holding[i], max(1, remaining * weights[i] // whole), rest)
            holding[i] = holding[i] + addition
            rest = rest - addition
    return np.array(holding)


def gaussian(key, dims, deviation, limit, pieces=(), held_as=jnp.bfloat16):
    loudness = levels(key, dims, pieces, -0.22, 0.18) if pieces else 1.0
    entries = jax.random.normal(key, dims, jnp.float32) * deviation * loudness
    return jnp.minimum(jnp.maximum(entries, -limit), limit).astype(held_as)


def setup_inputs(seed: int = 0) -> dict:
    key_list = jax.random.split(jax.random.key(seed), 7)
    pair_rows = gaussian(key_list[0], (TOKENS, D), 1.0, 6.0, ((0, 512),))
    group_ids_keys = jax.random.split(jax.random.fold_in(key_list[1], 1), TOKENS // ROWS_DEV)
    group_ids_turns = jax.random.permutation(jax.random.fold_in(key_list[1], 3), TOKENS // ROWS_DEV)
    group_ids = jax.vmap(lambda own, number: shared_out(jax.random.fold_in(key_list[1], 2), own, number, ROWS_DEV, N_GROUP, 1, GCAP, 2))(group_ids_keys, group_ids_turns).reshape((TOKENS, 1))
    local_ids = set_ends(jax.random.randint(key_list[2], (TOKENS, 1), 0, EXP_GROUP), jax.random.fold_in(key_list[2], 1), 0, EXP_GROUP - 1).astype(jnp.int32)
    route_weight = jnp.clip(jnp.exp(math.log(1.0) - 1.2039728 * jax.random.uniform(key_list[3], (TOKENS,), jnp.float32) ** levels(key_list[3], (TOKENS,), ((0, 512),), -0.2, 0.2)), 0.3, 1.0)
    w_up = gaussian(key_list[4], (EXPERTS, D, FF), D ** -0.5, 0.125, ((0, 16), (2, 32)))
    w_down = gaussian(key_list[5], (EXPERTS, FF, D), FF ** -0.5, 0.0625, ((0, 16), (1, 32)))
    return dict(pair_rows=pair_rows, group_ids=group_ids, local_ids=local_ids, route_weight=route_weight, w_up=w_up, w_down=w_down)


def reference(pair_rows, group_ids, local_ids, route_weight, w_up, w_down):
    expert_of = (group_ids[:, 0] * EXP_GROUP + local_ids[:, 0]).astype(jnp.int32)
    sorted_rows = jnp.argsort(expert_of, stable=True).astype(jnp.int32)
    counts = jnp.sum((expert_of[:, None] == jnp.arange(EXPERTS, dtype=jnp.int32)[None, :]).astype(jnp.int32), 0)
    starts = (jnp.cumsum(counts) - counts).astype(jnp.int32)
    most_rows = GCAP * N_GROUP * N_INNER
    padded = jnp.concatenate([sorted_rows, jnp.zeros((most_rows,), jnp.int32)])
    slice_width = FF // N_INNER

    def expert_step(expert, summed_out):
        start = starts[expert]
        row_index = lax.dynamic_slice_in_dim(padded, start, most_rows)
        is_valid = jnp.arange(most_rows, dtype=jnp.int32) < counts[expert]
        picked = pair_rows[row_index]
        up_val = jnp.dot(picked, w_up[expert], preferred_element_type=jnp.float32)
        hidden = jax.nn.silu(up_val).astype(jnp.bfloat16)
        down_mat = w_down[expert]

        def add_slice(running, which):
            hidden_part = lax.dynamic_slice_in_dim(hidden, which * slice_width, slice_width, 1)
            down_part = lax.dynamic_slice_in_dim(down_mat, which * slice_width, slice_width, 0)
            partial_value = jnp.dot(hidden_part, down_part, preferred_element_type=jnp.float32).astype(jnp.bfloat16)
            partial_value = lax.optimization_barrier(partial_value)
            return running + partial_value.astype(jnp.float32), None

        summed, _ = lax.scan(add_slice, jnp.zeros((most_rows, D), jnp.float32), jnp.arange(N_INNER, dtype=jnp.int32))
        summed = jnp.where(is_valid[:, None], summed, jnp.zeros_like(summed))
        return summed_out.at[row_index].add(summed)

    summed_out = lax.fori_loop(0, EXPERTS, expert_step, jnp.zeros((TOKENS, D), jnp.float32))
    expert_out = summed_out.astype(jnp.bfloat16)
    return (expert_out.astype(jnp.float32) * route_weight[:, None]).astype(jnp.bfloat16)
```

```python
import functools

import jax
import jax.numpy as jnp
from jax import lax
from jax.experimental import pallas as pl
from jax.experimental.pallas import tpu as pltpu
from jax.sharding import PartitionSpec as P

MESH = pl.DeviceIdType.MESH
XS, ZS = 4, 8
TAG = 128
f32, bf16 = jnp.float32, jnp.bfloat16


def kernel(
    rows_ref, gid_ref, lid_ref, rw_ref, wup_hbm, wdn_hbm, o_ref,
    wup, wdn, wsem,
    out_buf, in_buf, a2a_s, a2a_r,
    xa, xb, a1_s, a1_r, a2_s, a2_r, b1_s, b1_r, b2_s, b2_r,
    pa, pb, ra_s, ra_r, ra_buf, rax_s, rax_r, rax_out, rax_in,
    rbx_s, rbx_r, rbx_in, rb_s, rb_r, rb_buf, rb_out,
    ret_out, ret_in, ret_s, ret_r,
):
    n_rows, width = rows_ref.shape
    groups, cap = out_buf.shape[0], out_buf.shape[1]
    slots = groups * cap
    half = slots // 2
    g = lax.axis_index("group")
    i = lax.axis_index("inner")
    x, z = i // ZS, i % ZS

    def inner_at(xx, zz):
        return lax.rem(xx + XS, XS) * ZS + lax.rem(zz + ZS, ZS)

    right, left = inner_at(x, z + 1), inner_at(x, z - 1)

    def zat(d):
        return lax.rem(z + d + ZS, ZS)

    def xat(k):
        return lax.rem(x + k, XS)

    sent = []

    def send(src, dst, s, r, dev):
        c = pltpu.make_async_remote_copy(
            src_ref=src, dst_ref=dst, send_sem=s, recv_sem=r, device_id=dev, device_id_type=MESH
        )
        c.start()
        sent.append(c)

    def arrived(dst, s, r):
        pltpu.make_async_remote_copy(
            src_ref=dst, dst_ref=dst, send_sem=s, recv_sem=r, device_id=(g, right), device_id_type=MESH
        ).wait_recv()

    cw = [
        pltpu.make_async_copy(wup_hbm, wup, wsem.at[0]),
        pltpu.make_async_copy(wdn_hbm, wdn, wsem.at[1]),
    ]
    for c in cw:
        c.start()

    barrier = pltpu.get_barrier_semaphore()

    @pl.loop(1, groups)
    def _(k):
        pl.semaphore_signal(barrier, inc=1, device_id=(lax.rem(g + k, groups), i), device_id_type=MESH)

    for k in range(1, XS):
        pl.semaphore_signal(barrier, inc=1, device_id=(g, inner_at(x + k, z)), device_id_type=MESH)
    for dev in (right, left):
        pl.semaphore_signal(barrier, inc=1, device_id=(g, dev), device_id_type=MESH)

    gid = gid_ref[...]
    sub = lax.broadcasted_iota(jnp.int32, (n_rows, n_rows), 0)
    lane = lax.broadcasted_iota(jnp.int32, (n_rows, n_rows), 1)
    eye = sub == lane
    gcol = jnp.sum(jnp.where(eye, gid, 0), axis=1, keepdims=True)
    before_row = jnp.where((gcol == gid) & (sub < lane), 1, 0)
    target = gid * cap + jnp.sum(before_row, axis=0, keepdims=True)
    target_col = jnp.sum(jnp.where(eye, target, 0), axis=1, keepdims=True)
    places = lax.broadcasted_iota(jnp.int32, (slots, n_rows), 0) == target
    out_rows = jnp.dot(
        jnp.where(places, 1.0, 0.0).astype(bf16), rows_ref[...], preferred_element_type=f32
    ).astype(bf16)
    tags = jnp.sum(jnp.where(places, lid_ref[...], 0), axis=1, keepdims=True).astype(f32)
    out_tags = jnp.broadcast_to(tags, (slots, TAG)).astype(bf16)
    for d in range(groups):
        out_buf[d, :, :width] = out_rows[cap * d : cap * (d + 1)]
        out_buf[d, :, width:] = out_tags[cap * d : cap * (d + 1)]

    pl.semaphore_wait(barrier, groups - 1 + XS - 1 + 2)

    @pl.loop(1, groups)
    def _(k):
        d = lax.rem(g + k, groups)
        pltpu.make_async_remote_copy(
            src_ref=out_buf.at[d], dst_ref=in_buf.at[g], send_sem=a2a_s.at[d], recv_sem=a2a_r.at[g],
            device_id=(d, i), device_id_type=MESH,
        ).start()

    in_buf[g] = out_buf[g]

    @pl.loop(1, groups)
    def _(k):
        d = lax.rem(g + k, groups)
        arrived(in_buf.at[d], a2a_s.at[d], a2a_r.at[d])

    for d in range(groups // 2):
        xa[z, x, cap * d : cap * (d + 1), :] = in_buf[d]
        xb[x, z, cap * d : cap * (d + 1), :] = in_buf[d + groups // 2]

    def spread_b(zz):
        for k in range(1, XS):
            send(xb.at[x, zz], xb.at[x, zz], b2_s.at[k, zz], b2_r.at[x, zz], (g, inner_at(x + k, z)))

    send(xb.at[x, z], xb.at[x, z], b1_s.at[0, 0], b1_r.at[0, 0], (g, right))
    send(xb.at[x, z], xb.at[x, z], b1_s.at[1, 0], b1_r.at[1, 0], (g, left))
    for k in range(1, XS):
        send(xa.at[z, x], xa.at[z, x], a1_s.at[k], a1_r.at[x], (g, inner_at(x + k, z)))
    spread_b(z)
    for k in range(1, XS):
        arrived(xa.at[z, xat(k)], a1_s.at[k], a1_r.at[xat(k)])

    def ring_a(step):
        for p in range(2):
            if step < 3 or p == 0:
                blk = xa.at[zat(-step), pl.ds(2 * p, 2)]
                send(blk, blk, a2_s.at[0, step, p], a2_r.at[0, step, p], (g, right))
            if step < 3 or p == 1:
                blk = xa.at[zat(step), pl.ds(2 * p, 2)]
                send(blk, blk, a2_s.at[1, step, p], a2_r.at[1, step, p], (g, left))

    def came_a(step):
        for p in range(2):
            if step < 4 or p == 0:
                arrived(xa.at[zat(-step), pl.ds(2 * p, 2)], a2_s.at[0, step - 1, p], a2_r.at[0, step - 1, p])
            if step < 4 or p == 1:
                arrived(xa.at[zat(step), pl.ds(2 * p, 2)], a2_s.at[1, step - 1, p], a2_r.at[1, step - 1, p])

    ring_a(0)
    for c in cw:
        c.wait()

    def experts(val):
        tag = val[:, width:].astype(f32)
        out = None
        for e in range(2):
            up = jnp.dot(val[:, :width], wup[e], preferred_element_type=f32)
            hid = up / (1.0 + jnp.exp(-up))
            mask = jnp.where(tag == float(e), 1.0, 0.0)
            hid = (hid * jnp.concatenate([mask] * (hid.shape[1] // TAG), axis=1)).astype(bf16)
            part = jnp.dot(hid, wdn[e], preferred_element_type=f32)
            out = part if out is None else out + part
        return out.astype(bf16)

    def compute_b(xx):
        val = xb[xx].reshape(ZS * half, width + TAG)
        pb[xx] = experts(val).reshape(ZS, half, width)

    def compute_a(z0, z1):
        val = jnp.concatenate(
            [xa[z0].reshape(XS * half, width + TAG), xa[z1].reshape(XS * half, width + TAG)], axis=0
        )
        out = experts(val).reshape(2, XS, half, width)
        pa[z0] = out[0]
        pa[z1] = out[1]

    for step in range(1, 5):
        arrived(xb.at[x, zat(-step)], b1_s.at[0, step - 1], b1_r.at[0, step - 1])
        if step < 4:
            send(xb.at[x, zat(-step)], xb.at[x, zat(-step)], b1_s.at[0, step], b1_r.at[0, step], (g, right))
            arrived(xb.at[x, zat(step)], b1_s.at[1, step - 1], b1_r.at[1, step - 1])
        if step < 3:
            send(xb.at[x, zat(step)], xb.at[x, zat(step)], b1_s.at[1, step], b1_r.at[1, step], (g, left))
        spread_b(zat(-step))
        if step < 4:
            spread_b(zat(step))
    compute_b(x)
    for step in range(1, 5):
        came_a(step)
        if step < 4:
            ring_a(step)
            if step > 1:
                compute_a(zat(step - 1), zat(1 - step))
    compute_a(zat(3), zat(-3))
    compute_a(z, zat(4))

    def add_a(way, step, zz, xs):
        ra_buf[way, step, xs] = (ra_buf[way, step, xs].astype(f32) + pa[zz, xs].astype(f32)).astype(bf16)

    xlo, xhi = pl.ds(0, 2), pl.ds(2, 2)
    send(pa.at[zat(4), xlo], ra_buf.at[0, 0, xlo], ra_s.at[0, 0, 0], ra_r.at[0, 0, 0], (g, right))
    send(pa.at[zat(4), xhi], ra_buf.at[1, 0, xhi], ra_s.at[1, 0, 1], ra_r.at[1, 0, 1], (g, left))
    send(pa.at[zat(3), xhi], ra_buf.at[0, 1, xhi], ra_s.at[0, 1, 1], ra_r.at[0, 1, 1], (g, right))
    send(pa.at[zat(-3), xlo], ra_buf.at[1, 1, xlo], ra_s.at[1, 1, 0], ra_r.at[1, 1, 0], (g, left))

    order = [4, 3, -3, 2, -2, 1, -1, 0]
    for k in range(1, XS):
        xx = xat(k)
        for zd in range(ZS):
            arrived(xb.at[xx, zat(zd)], b2_s.at[k, zat(zd)], b2_r.at[xx, zat(zd)])
        compute_b(xx)
        for zd in order:
            zz = zat(zd)
            send(pb.at[xx, zz], rbx_in.at[x, zz], rbx_s.at[k, zz], rbx_r.at[x, zz], (g, inner_at(x + k, z)))

    def ring_ra(step):
        for way, sgn, dev in ((0, 1, right), (1, -1, left)):
            for p in range(2):
                if step == 1 and p != way:
                    continue
                xs = pl.ds(2 * p, 2)
                arrived(ra_buf.at[way, step - 1, xs], ra_s.at[way, step - 1, p], ra_r.at[way, step - 1, p])
                if step < 4:
                    add_a(way, step - 1, zat(sgn * (4 - step)), xs)
                    send(ra_buf.at[way, step - 1, xs], ra_buf.at[way, step, xs], ra_s.at[way, step, p], ra_r.at[way, step, p], (g, dev))

    def col_sum(zz):
        tot = pb[x, zz].astype(f32)
        for k in range(1, XS):
            arrived(rbx_in.at[xat(k), zz], rbx_s.at[k, zz], rbx_r.at[xat(k), zz])
            tot = tot + rbx_in[xat(k), zz].astype(f32)
        return tot

    for step in range(1, 5):
        ring_ra(step)

    for xx in range(XS):
        rax_out[xx] = (
            pa[z, xx].astype(f32) + ra_buf[0, 3, xx].astype(f32) + ra_buf[1, 3, xx].astype(f32)
        ).astype(bf16)
    for k in range(1, XS):
        send(rax_out.at[xat(k)], rax_in.at[x], rax_s.at[k], rax_r.at[x], (g, inner_at(x + k, z)))

    rb_out[0, 0] = col_sum(zat(4)).astype(bf16)
    send(rb_out.at[0, 0], rb_buf.at[0, 0], rb_s.at[0, 0], rb_r.at[0, 0], (g, right))
    rb_out[1, 0] = col_sum(zat(-3)).astype(bf16)
    send(rb_out.at[1, 0], rb_buf.at[1, 0], rb_s.at[1, 0], rb_r.at[1, 0], (g, left))
    for step in range(1, 4):
        own = col_sum(zat(4 - step))
        arrived(rb_buf.at[0, step - 1], rb_s.at[0, step - 1], rb_r.at[0, step - 1])
        rb_out[0, step] = (own + rb_buf[0, step - 1].astype(f32)).astype(bf16)
        send(rb_out.at[0, step], rb_buf.at[0, step], rb_s.at[0, step], rb_r.at[0, step], (g, right))
        if step < 3:
            own = col_sum(zat(-3 + step))
            arrived(rb_buf.at[1, step - 1], rb_s.at[1, step - 1], rb_r.at[1, step - 1])
            rb_out[1, step] = (own + rb_buf[1, step - 1].astype(f32)).astype(bf16)
            send(rb_out.at[1, step], rb_buf.at[1, step], rb_s.at[1, step], rb_r.at[1, step], (g, left))

    tot = rax_out[x].astype(f32)
    for k in range(1, XS):
        arrived(rax_in.at[xat(k)], rax_s.at[k], rax_r.at[xat(k)])
        tot = tot + rax_in[xat(k)].astype(f32)
    fin = tot.astype(bf16)
    for d in range(groups // 2):
        ret_out[d] = fin[cap * d : cap * (d + 1)]
    tot = col_sum(z)
    for way, step in ((1, 2), (0, 3)):
        arrived(rb_buf.at[way, step], rb_s.at[way, step], rb_r.at[way, step])
        tot = tot + rb_buf[way, step].astype(f32)
    fin = tot.astype(bf16)
    for d in range(groups // 2):
        ret_out[d + groups // 2] = fin[cap * d : cap * (d + 1)]

    @pl.loop(1, groups)
    def _(k):
        d = lax.rem(g + k, groups)
        pltpu.make_async_remote_copy(
            src_ref=ret_out.at[d], dst_ref=ret_in.at[g], send_sem=ret_s.at[d], recv_sem=ret_r.at[g],
            device_id=(d, i), device_id_type=MESH,
        ).start()

    ret_in[g] = ret_out[g]

    @pl.loop(1, groups)
    def _(k):
        d = lax.rem(g + k, groups)
        arrived(ret_in.at[d], ret_s.at[d], ret_r.at[d])

    returned = jnp.concatenate([ret_in[d] for d in range(groups)], axis=0)
    places_t = lax.broadcasted_iota(jnp.int32, (n_rows, slots), 1) == target_col
    combined = jnp.dot(jnp.where(places_t, 1.0, 0.0).astype(bf16), returned, preferred_element_type=f32)
    rw = jnp.sum(jnp.where(eye, rw_ref[...], 0.0), axis=1, keepdims=True)
    o_ref[...] = (combined * rw).astype(o_ref.dtype)

    for c in sent:
        c.wait_send()

    @pl.loop(1, groups)
    def _(k):
        d = lax.rem(g + k, groups)
        for src, dst, s, r in ((out_buf, in_buf, a2a_s, a2a_r), (ret_out, ret_in, ret_s, ret_r)):
            pltpu.make_async_remote_copy(
                src_ref=src.at[d], dst_ref=dst.at[g], send_sem=s.at[d], recv_sem=r.at[g],
                device_id=(d, i), device_id_type=MESH,
            ).wait_send()


def body(pair_rows, group_ids, local_ids, route_weight, w_up, w_down):
    groups = lax.axis_size("group")
    n_rows, width = pair_rows.shape
    cap = 2 * n_rows // groups
    half = groups * cap // 2
    wide = width + TAG
    dma = pltpu.SemaphoreType.DMA
    vmem, hbm = pl.BlockSpec(memory_space=pltpu.VMEM), pl.BlockSpec(memory_space=pl.ANY)
    V = pltpu.VMEM
    scratch = [
        V(w_up.shape, bf16), V(w_down.shape, bf16), dma((2,)),
        V((groups, cap, wide), bf16), V((groups, cap, wide), bf16), dma((groups,)), dma((groups,)),
        V((ZS, XS, half, wide), bf16), V((XS, ZS, half, wide), bf16),
        dma((XS,)), dma((XS,)), dma((2, 4, 2)), dma((2, 4, 2)), dma((2, 4)), dma((2, 4)), dma((XS, ZS)), dma((XS, ZS)),
        V((ZS, XS, half, width), bf16), V((XS, ZS, half, width), bf16),
        dma((2, 4, 2)), dma((2, 4, 2)), V((2, 4, XS, half, width), bf16), dma((XS,)), dma((XS,)),
        V((XS, half, width), bf16), V((XS, half, width), bf16),
        dma((XS, ZS)), dma((XS, ZS)), V((XS, ZS, half, width), bf16),
        dma((2, 4)), dma((2, 4)), V((2, 4, half, width), bf16), V((2, 4, half, width), bf16),
        V((groups, cap, width), bf16), V((groups, cap, width), bf16), dma((groups,)), dma((groups,)),
    ]
    return pl.pallas_call(
        kernel,
        out_shape=jax.ShapeDtypeStruct((n_rows, width), bf16),
        in_specs=[vmem] * 4 + [hbm] * 2,
        out_specs=vmem,
        scratch_shapes=scratch,
        compiler_params=pltpu.CompilerParams(
            collective_id=0, has_side_effects=True, vmem_limit_bytes=56 * 2**20
        ),
        name="routed_experts",
    )(
        pair_rows,
        group_ids.reshape(1, n_rows),
        local_ids.reshape(1, n_rows),
        route_weight.reshape(1, n_rows),
        w_up,
        w_down,
    )


def solution(mesh):
    placed = (
        P(("group", "inner"), None),
        P(("group", "inner"), None),
        P(("group", "inner"), None),
        P(("group", "inner")),
        P("group", None, "inner"),
        P("group", "inner", None),
    )
    return jax.shard_map(
        body, mesh=mesh, in_specs=placed, out_specs=P(("group", "inner"), None), check_vma=False
    )
```

```python
import functools

import jax
import jax.numpy as jnp
from jax import lax
from jax.experimental import pallas as pl
from jax.experimental.pallas import tpu as pltpu
from jax.sharding import PartitionSpec as P

MESH = pl.DeviceIdType.MESH
XS, ZS = 4, 8
TAG = 128
f32, bf16 = jnp.float32, jnp.bfloat16


def kernel(
    rows_ref, gid_ref, lid_ref, rw_ref, wup_hbm, wdn_hbm, o_ref,
    wup, wdn, wsem,
    out_buf, in_buf, a2a_s, a2a_r,
    xs, a1_s, a1_r, a2_s, a2_r, b1_s, b1_r, b2_s, b2_r,
    ps, ra_s, ra_r, ra_buf, rax_s, rax_r, rax_out, rax_in,
    rbx_s, rbx_r, rbx_in, rb_s, rb_r, rb_buf, rb_out,
    ret_out, ret_in, ret_s, ret_r,
):
    n_rows, width = rows_ref.shape
    groups, cap = out_buf.shape[0], out_buf.shape[1]
    slots = groups * cap
    half = slots // 2
    g = lax.axis_index("group")
    i = lax.axis_index("inner")
    x, z = i // ZS, i % ZS

    def inner_at(xx, zz):
        return lax.rem(xx + XS, XS) * ZS + lax.rem(zz + ZS, ZS)

    right, left = inner_at(x, z + 1), inner_at(x, z - 1)

    def zat(d):
        return lax.rem(z + d + ZS, ZS)

    def xat(k):
        return lax.rem(x + k, XS)

    sent = []

    def send(src, dst, s, r, dev):
        c = pltpu.make_async_remote_copy(
            src_ref=src, dst_ref=dst, send_sem=s, recv_sem=r, device_id=dev, device_id_type=MESH
        )
        c.start()
        sent.append(c)

    def arrived(dst, s, r):
        pltpu.make_async_remote_copy(
            src_ref=dst, dst_ref=dst, send_sem=s, recv_sem=r, device_id=(g, right), device_id_type=MESH
        ).wait_recv()

    cw = [
        pltpu.make_async_copy(wup_hbm, wup, wsem.at[0]),
        pltpu.make_async_copy(wdn_hbm, wdn, wsem.at[1]),
    ]
    for c in cw:
        c.start()

    barrier = pltpu.get_barrier_semaphore()

    @pl.loop(1, groups)
    def _(k):
        pl.semaphore_signal(barrier, inc=1, device_id=(lax.rem(g + k, groups), i), device_id_type=MESH)

    for k in range(1, XS):
        pl.semaphore_signal(barrier, inc=1, device_id=(g, inner_at(x + k, z)), device_id_type=MESH)
    for dev in (right, left):
        pl.semaphore_signal(barrier, inc=1, device_id=(g, dev), device_id_type=MESH)

    gid = gid_ref[...]
    sub = lax.broadcasted_iota(jnp.int32, (n_rows, n_rows), 0)
    lane = lax.broadcasted_iota(jnp.int32, (n_rows, n_rows), 1)
    eye = sub == lane
    gcol = jnp.sum(jnp.where(eye, gid, 0), axis=1, keepdims=True)
    before_row = jnp.where((gcol == gid) & (sub < lane), 1, 0)
    target = gid * cap + jnp.sum(before_row, axis=0, keepdims=True)
    target_col = jnp.sum(jnp.where(eye, target, 0), axis=1, keepdims=True)
    places = lax.broadcasted_iota(jnp.int32, (slots, n_rows), 0) == target
    out_rows = jnp.dot(
        jnp.where(places, 1.0, 0.0).astype(bf16), rows_ref[...], preferred_element_type=f32
    ).astype(bf16)
    tags = jnp.sum(jnp.where(places, lid_ref[...], 0), axis=1, keepdims=True).astype(f32)
    out_tags = jnp.broadcast_to(tags, (slots, TAG)).astype(bf16)
    for d in range(groups):
        out_buf[d, :, :width] = out_rows[cap * d : cap * (d + 1)]
        out_buf[d, :, width:] = out_tags[cap * d : cap * (d + 1)]

    pl.semaphore_wait(barrier, groups - 1 + XS - 1 + 2)

    @pl.loop(1, groups)
    def _(k):
        d = lax.rem(g + k, groups)
        pltpu.make_async_remote_copy(
            src_ref=out_buf.at[d], dst_ref=in_buf.at[g], send_sem=a2a_s.at[d], recv_sem=a2a_r.at[g],
            device_id=(d, i), device_id_type=MESH,
        ).start()

    in_buf[g] = out_buf[g]

    @pl.loop(1, groups)
    def _(k):
        d = lax.rem(g + k, groups)
        arrived(in_buf.at[d], a2a_s.at[d], a2a_r.at[d])

    for d in range(groups // 2):
        xs[z, 0, x, cap * d : cap * (d + 1), :] = in_buf[d]
        xs[z, 1, x, cap * d : cap * (d + 1), :] = in_buf[d + groups // 2]

    def spread_b(zz):
        for k in range(1, XS):
            send(xs.at[zz, 1, x], xs.at[zz, 1, x], b2_s.at[k, zz], b2_r.at[x, zz], (g, inner_at(x + k, z)))

    def ring_b(step):
        blk = xs.at[zat(-step), 1, x]
        send(blk, blk, b1_s.at[0, step], b1_r.at[0, step], (g, right))
        if step < 3:
            blk = xs.at[zat(step), 1, x]
            send(blk, blk, b1_s.at[1, step], b1_r.at[1, step], (g, left))

    def came_b(step):
        arrived(xs.at[zat(-step), 1, x], b1_s.at[0, step - 1], b1_r.at[0, step - 1])
        if step < 4:
            arrived(xs.at[zat(step), 1, x], b1_s.at[1, step - 1], b1_r.at[1, step - 1])

    def came_cols(zz):
        for k in range(1, XS):
            arrived(xs.at[zz, 1, xat(k)], b2_s.at[k, zz], b2_r.at[xat(k), zz])

    def ring_a(step):
        for p in range(2):
            if step < 3 or p == 0:
                blk = xs.at[zat(-step), 0, pl.ds(2 * p, 2)]
                send(blk, blk, a2_s.at[0, step, p], a2_r.at[0, step, p], (g, right))
            if step < 3 or p == 1:
                blk = xs.at[zat(step), 0, pl.ds(2 * p, 2)]
                send(blk, blk, a2_s.at[1, step, p], a2_r.at[1, step, p], (g, left))

    def came_a(step):
        for p in range(2):
            if step < 4 or p == 0:
                arrived(xs.at[zat(-step), 0, pl.ds(2 * p, 2)], a2_s.at[0, step - 1, p], a2_r.at[0, step - 1, p])
            if step < 4 or p == 1:
                arrived(xs.at[zat(step), 0, pl.ds(2 * p, 2)], a2_s.at[1, step - 1, p], a2_r.at[1, step - 1, p])

    def experts(val):
        tag = val[:, width:].astype(f32)
        out = None
        for e in range(2):
            up = jnp.dot(val[:, :width], wup[e], preferred_element_type=f32)
            hid = up / (1.0 + jnp.exp(-up))
            mask = jnp.where(tag == float(e), 1.0, 0.0)
            hid = (hid * jnp.concatenate([mask] * (hid.shape[1] // TAG), axis=1)).astype(bf16)
            part = jnp.dot(hid, wdn[e], preferred_element_type=f32)
            out = part if out is None else out + part
        return out.astype(bf16)

    def compute(zz):
        ps[zz] = experts(xs[zz].reshape(2 * XS * half, width + TAG)).reshape(2, XS, half, width)

    def compute_half(zz, h):
        ps[zz, h] = experts(xs[zz, h].reshape(XS * half, width + TAG)).reshape(XS, half, width)

    def sum_pieces(zz):
        for k in range(1, XS):
            send(ps.at[zz, 1, xat(k)], rbx_in.at[x, zz], rbx_s.at[k, zz], rbx_r.at[x, zz], (g, inner_at(x + k, z)))

    ring_b(0)
    for k in range(1, XS):
        send(xs.at[z, 0, x], xs.at[z, 0, x], a1_s.at[k], a1_r.at[x], (g, inner_at(x + k, z)))
    spread_b(z)
    for k in range(1, XS):
        arrived(xs.at[z, 0, xat(k)], a1_s.at[k], a1_r.at[xat(k)])
    ring_a(0)
    for c in cw:
        c.wait()
    for step in range(1, 4):
        came_b(step)
        ring_b(step)
        spread_b(zat(-step))
        spread_b(zat(step))
        came_a(step)
        ring_a(step)
        for zd in sorted({step - 1, 1 - step}):
            came_cols(zat(zd))
            compute(zat(zd))
    came_b(4)
    spread_b(zat(4))
    for zd in (3, -3):
        came_cols(zat(zd))
        compute(zat(zd))
    for zd in (0, 1, -1):
        sum_pieces(zat(zd))
    came_a(4)
    compute_half(zat(4), 0)

    def add_a(way, step, zz, sl):
        ra_buf[way, step, sl] = (ra_buf[way, step, sl].astype(f32) + ps[zz, 0, sl].astype(f32)).astype(bf16)

    lo, hi = pl.ds(0, 2), pl.ds(2, 2)
    send(ps.at[zat(4), 0, lo], ra_buf.at[0, 0, lo], ra_s.at[0, 0, 0], ra_r.at[0, 0, 0], (g, right))
    send(ps.at[zat(4), 0, hi], ra_buf.at[1, 0, hi], ra_s.at[1, 0, 1], ra_r.at[1, 0, 1], (g, left))
    send(ps.at[zat(3), 0, hi], ra_buf.at[0, 1, hi], ra_s.at[0, 1, 1], ra_r.at[0, 1, 1], (g, right))
    send(ps.at[zat(-3), 0, lo], ra_buf.at[1, 1, lo], ra_s.at[1, 1, 0], ra_r.at[1, 1, 0], (g, left))

    came_cols(zat(4))
    compute_half(zat(4), 1)
    for zd in (4, 3, -3, 2, -2):
        sum_pieces(zat(zd))

    def ring_ra(step):
        for p in range(2):
            for way, sgn, dev in ((0, 1, right), (1, -1, left)):
                if step == 1 and p != way:
                    continue
                sl = pl.ds(2 * p, 2)
                arrived(ra_buf.at[way, step - 1, sl], ra_s.at[way, step - 1, p], ra_r.at[way, step - 1, p])
                if step < 4:
                    add_a(way, step - 1, zat(sgn * (4 - step)), sl)
                    send(ra_buf.at[way, step - 1, sl], ra_buf.at[way, step, sl], ra_s.at[way, step, p], ra_r.at[way, step, p], (g, dev))

    def col_sum(zz):
        tot = ps[zz, 1, x].astype(f32)
        for k in range(1, XS):
            arrived(rbx_in.at[xat(k), zz], rbx_s.at[k, zz], rbx_r.at[xat(k), zz])
            tot = tot + rbx_in[xat(k), zz].astype(f32)
        return tot

    def ring_rb(way, step, zz, dev):
        tot = col_sum(zz)
        if step > 0:
            arrived(rb_buf.at[way, step - 1], rb_s.at[way, step - 1], rb_r.at[way, step - 1])
            tot = tot + rb_buf[way, step - 1].astype(f32)
        rb_out[way, step] = tot.astype(bf16)
        send(rb_out.at[way, step], rb_buf.at[way, step], rb_s.at[way, step], rb_r.at[way, step], (g, dev))

    for step in range(1, 4):
        ring_ra(step)
        ring_rb(0, step - 1, zat(5 - step), right)
        ring_rb(1, step - 1, zat(step - 4), left)
    ring_ra(4)

    for xx in range(XS):
        rax_out[xx] = (
            ps[z, 0, xx].astype(f32) + ra_buf[0, 3, xx].astype(f32) + ra_buf[1, 3, xx].astype(f32)
        ).astype(bf16)
    for k in range(1, XS):
        send(rax_out.at[xat(k)], rax_in.at[x], rax_s.at[k], rax_r.at[x], (g, inner_at(x + k, z)))
    ring_rb(0, 3, zat(1), right)

    tot = rax_out[x].astype(f32)
    for k in range(1, XS):
        arrived(rax_in.at[xat(k)], rax_s.at[k], rax_r.at[xat(k)])
        tot = tot + rax_in[xat(k)].astype(f32)
    fin = tot.astype(bf16)
    for d in range(groups // 2):
        ret_out[d] = fin[cap * d : cap * (d + 1)]
    tot = col_sum(z)
    for way, step in ((1, 2), (0, 3)):
        arrived(rb_buf.at[way, step], rb_s.at[way, step], rb_r.at[way, step])
        tot = tot + rb_buf[way, step].astype(f32)
    fin = tot.astype(bf16)
    for d in range(groups // 2):
        ret_out[d + groups // 2] = fin[cap * d : cap * (d + 1)]

    @pl.loop(1, groups)
    def _(k):
        d = lax.rem(g + k, groups)
        pltpu.make_async_remote_copy(
            src_ref=ret_out.at[d], dst_ref=ret_in.at[g], send_sem=ret_s.at[d], recv_sem=ret_r.at[g],
            device_id=(d, i), device_id_type=MESH,
        ).start()

    ret_in[g] = ret_out[g]

    @pl.loop(1, groups)
    def _(k):
        d = lax.rem(g + k, groups)
        arrived(ret_in.at[d], ret_s.at[d], ret_r.at[d])

    returned = jnp.concatenate([ret_in[d] for d in range(groups)], axis=0)
    places_t = lax.broadcasted_iota(jnp.int32, (n_rows, slots), 1) == target_col
    combined = jnp.dot(jnp.where(places_t, 1.0, 0.0).astype(bf16), returned, preferred_element_type=f32)
    rw = jnp.sum(jnp.where(eye, rw_ref[...], 0.0), axis=1, keepdims=True)
    o_ref[...] = (combined * rw).astype(o_ref.dtype)

    for c in sent:
        c.wait_send()

    @pl.loop(1, groups)
    def _(k):
        d = lax.rem(g + k, groups)
        for src, dst, s, r in ((out_buf, in_buf, a2a_s, a2a_r), (ret_out, ret_in, ret_s, ret_r)):
            pltpu.make_async_remote_copy(
                src_ref=src.at[d], dst_ref=dst.at[g], send_sem=s.at[d], recv_sem=r.at[g],
                device_id=(d, i), device_id_type=MESH,
            ).wait_send()


def body(pair_rows, group_ids, local_ids, route_weight, w_up, w_down):
    groups = lax.axis_size("group")
    n_rows, width = pair_rows.shape
    cap = 2 * n_rows // groups
    half = groups * cap // 2
    wide = width + TAG
    dma = pltpu.SemaphoreType.DMA
    vmem, hbm = pl.BlockSpec(memory_space=pltpu.VMEM), pl.BlockSpec(memory_space=pl.ANY)
    V = pltpu.VMEM
    scratch = [
        V(w_up.shape, bf16), V(w_down.shape, bf16), dma((2,)),
        V((groups, cap, wide), bf16), V((groups, cap, wide), bf16), dma((groups,)), dma((groups,)),
        V((ZS, 2, XS, half, wide), bf16),
        dma((XS,)), dma((XS,)), dma((2, 4, 2)), dma((2, 4, 2)), dma((2, 4)), dma((2, 4)), dma((XS, ZS)), dma((XS, ZS)),
        V((ZS, 2, XS, half, width), bf16),
        dma((2, 4, 2)), dma((2, 4, 2)), V((2, 4, XS, half, width), bf16), dma((XS,)), dma((XS,)),
        V((XS, half, width), bf16), V((XS, half, width), bf16),
        dma((XS, ZS)), dma((XS, ZS)), V((XS, ZS, half, width), bf16),
        dma((2, 4)), dma((2, 4)), V((2, 4, half, width), bf16), V((2, 4, half, width), bf16),
        V((groups, cap, width), bf16), V((groups, cap, width), bf16), dma((groups,)), dma((groups,)),
    ]
    return pl.pallas_call(
        kernel,
        out_shape=jax.ShapeDtypeStruct((n_rows, width), bf16),
        in_specs=[vmem] * 4 + [hbm] * 2,
        out_specs=vmem,
        scratch_shapes=scratch,
        compiler_params=pltpu.CompilerParams(
            collective_id=0, has_side_effects=True, vmem_limit_bytes=56 * 2**20
        ),
        name="routed_experts",
    )(
        pair_rows,
        group_ids.reshape(1, n_rows),
        local_ids.reshape(1, n_rows),
        route_weight.reshape(1, n_rows),
        w_up,
        w_down,
    )


def solution(mesh):
    placed = (
        P(("group", "inner"), None),
        P(("group", "inner"), None),
        P(("group", "inner"), None),
        P(("group", "inner")),
        P("group", None, "inner"),
        P("group", "inner", None),
    )
    return jax.shard_map(
        body, mesh=mesh, in_specs=placed, out_specs=P(("group", "inner"), None), check_vma=False
    )
```

```python
import functools

import jax
import jax.numpy as jnp
from jax import lax
from jax.experimental import pallas as pl
from jax.experimental.pallas import tpu as pltpu
from jax.sharding import PartitionSpec as P

MESH = pl.DeviceIdType.MESH
XS, ZS = 4, 8
TAG = 128
f32, bf16 = jnp.float32, jnp.bfloat16


def kernel(
    rows_ref, gid_ref, lid_ref, rw_ref, wup_hbm, wdn_hbm, o_ref,
    wup, wdn, wsem,
    out_buf, in_buf, a2a_s, a2a_r,
    xa, xb, a1_s, a1_r, a2_s, a2_r, b1_s, b1_r, b2_s, b2_r,
    pa, pb, ra_s, ra_r, ra_buf, rax_s, rax_r, rax_out, rax_in,
    cx_s, cx_r, cx_in, cx_out, rb_s, rb_r, rb_buf, rb_out,
    ret_out, ret_in, ret_s, ret_r,
):
    n_rows, width = rows_ref.shape
    groups, cap = out_buf.shape[0], out_buf.shape[1]
    slots = groups * cap
    half = slots // 2
    wa = xa.shape[-1]
    g = lax.axis_index("group")
    i = lax.axis_index("inner")
    x, z = i // ZS, i % ZS

    def inner_at(xx, zz):
        return lax.rem(xx + XS, XS) * ZS + lax.rem(zz + ZS, ZS)

    right, left = inner_at(x, z + 1), inner_at(x, z - 1)

    def zat(d):
        return lax.rem(z + d + ZS, ZS)

    def xat(k):
        return lax.rem(x + k, XS)

    sent = []

    def send(src, dst, s, r, dev):
        c = pltpu.make_async_remote_copy(
            src_ref=src, dst_ref=dst, send_sem=s, recv_sem=r, device_id=dev, device_id_type=MESH
        )
        c.start()
        sent.append(c)

    def arrived(dst, s, r):
        pltpu.make_async_remote_copy(
            src_ref=dst, dst_ref=dst, send_sem=s, recv_sem=r, device_id=(g, right), device_id_type=MESH
        ).wait_recv()

    cw = [
        pltpu.make_async_copy(wup_hbm, wup, wsem.at[0]),
        pltpu.make_async_copy(wdn_hbm, wdn, wsem.at[1]),
    ]
    for c in cw:
        c.start()

    barrier = pltpu.get_barrier_semaphore()

    @pl.loop(1, groups)
    def _(k):
        pl.semaphore_signal(barrier, inc=1, device_id=(lax.rem(g + k, groups), i), device_id_type=MESH)

    for k in range(1, XS):
        pl.semaphore_signal(barrier, inc=1, device_id=(g, inner_at(x + k, z)), device_id_type=MESH)
    for dev in (right, left):
        pl.semaphore_signal(barrier, inc=1, device_id=(g, dev), device_id_type=MESH)

    gid = gid_ref[...]
    sub = lax.broadcasted_iota(jnp.int32, (n_rows, n_rows), 0)
    lane = lax.broadcasted_iota(jnp.int32, (n_rows, n_rows), 1)
    eye = sub == lane
    gcol = jnp.sum(jnp.where(eye, gid, 0), axis=1, keepdims=True)
    before_row = jnp.where((gcol == gid) & (sub < lane), 1, 0)
    target = gid * cap + jnp.sum(before_row, axis=0, keepdims=True)
    target_col = jnp.sum(jnp.where(eye, target, 0), axis=1, keepdims=True)
    places = lax.broadcasted_iota(jnp.int32, (slots, n_rows), 0) == target
    out_rows = jnp.dot(
        jnp.where(places, 1.0, 0.0).astype(bf16), rows_ref[...], preferred_element_type=f32
    ).astype(bf16)
    tags = jnp.sum(jnp.where(places, lid_ref[...], 0), axis=1, keepdims=True).astype(f32)
    out_tags = jnp.broadcast_to(tags, (slots, TAG)).astype(bf16)
    for d in range(groups):
        out_buf[d, :, :width] = out_rows[cap * d : cap * (d + 1)]
        out_buf[d, :, width:] = out_tags[cap * d : cap * (d + 1)]

    pl.semaphore_wait(barrier, groups - 1 + XS - 1 + 2)

    def far_first(j):
        return lax.rem(g + groups // 2 + (2 * lax.rem(j, 2) - 1) * (j // 2), groups)

    @pl.loop(1, groups)
    def _(j):
        d = far_first(j)
        pltpu.make_async_remote_copy(
            src_ref=out_buf.at[d], dst_ref=in_buf.at[g], send_sem=a2a_s.at[d], recv_sem=a2a_r.at[g],
            device_id=(d, i), device_id_type=MESH,
        ).start()

    in_buf[g] = out_buf[g]

    @pl.loop(1, groups)
    def _(k):
        d = lax.rem(g + k, groups)
        arrived(in_buf.at[d], a2a_s.at[d], a2a_r.at[d])

    for d in range(groups):
        xa[z, x, cap * d : cap * (d + 1), :] = in_buf[d, :, :wa]
        xb[z, x, cap * d : cap * (d + 1), :] = in_buf[d, :, wa:]

    near = (1, 3, 2)
    last = ((0, 1), (3, 2))
    xr, xl = inner_at(x + 1, z), inner_at(x - 1, z)
    rows_of = (pl.ds(0, half), pl.ds(half, half))
    ways = ((0, -1, right), (1, 1, left))

    def passed_on(zd):
        return (3, 1, xr) if zd in (0, -1, -2, -3) else (1, 3, xl)

    def spread_b(zd):
        blk = xb.at[zat(zd), x]
        send(blk, blk, b2_s.at[1, zat(zd)], b2_r.at[x, zat(zd)], (g, xr))
        send(blk, blk, b2_s.at[3, zat(zd)], b2_r.at[x, zat(zd)], (g, xl))

    def came_col(zd, k):
        arrived(xb.at[zat(zd), xat(k)], b2_s.at[2, zat(zd)], b2_r.at[xat(k), zat(zd)])

    def relay_b(zd):
        k, _, dev = passed_on(zd)
        came_col(zd, k)
        blk = xb.at[zat(zd), xat(k)]
        send(blk, blk, b2_s.at[2, zat(zd)], b2_r.at[xat(k), zat(zd)], (g, dev))

    def came_cols(zd):
        came_col(zd, passed_on(zd)[1])
        came_col(zd, 2)

    def ring_b(step):
        for way, sgn, dev in ways:
            blk = xb.at[zat(sgn * step), x]
            if step == 3:
                blk = blk.at[rows_of[way]]
            send(blk, blk, b1_s.at[way, step], b1_r.at[way, step], (g, dev))

    def came_b(step):
        for way, sgn, _ in ways:
            blk = xb.at[zat(sgn * step), x]
            if step == 4:
                blk = blk.at[rows_of[way]]
            arrived(blk, b1_s.at[way, step - 1], b1_r.at[way, step - 1])

    def ring_a(step, k):
        for way, sgn, dev in ways:
            if step < 3 or k in last[way]:
                blk = xa.at[zat(sgn * step), xat(k)]
                send(blk, blk, a2_s.at[way, step, k], a2_r.at[way, step, k], (g, dev))

    def came_a(step, k):
        for way, sgn, _ in ways:
            if step < 4 or k in last[way]:
                arrived(xa.at[zat(sgn * step), xat(k)], a2_s.at[way, step - 1, k], a2_r.at[way, step - 1, k])

    def compute(zd):
        zz = zat(zd)
        va = xa[zz].reshape(XS * slots, wa)
        vb = xb[zz].reshape(XS * slots, width - wa + TAG)
        tag = vb[:, width - wa :].astype(f32)
        out = None
        for e in range(2):
            up = jnp.dot(va, wup[e, :wa], preferred_element_type=f32)
            up = up + jnp.dot(vb[:, : width - wa], wup[e, wa:], preferred_element_type=f32)
            hid = up / (1.0 + jnp.exp(-up))
            mask = jnp.where(tag == float(e), 1.0, 0.0)
            hid = (hid * jnp.concatenate([mask] * (hid.shape[1] // TAG), axis=1)).astype(bf16)
            part = jnp.dot(hid, wdn[e], preferred_element_type=f32)
            out = part if out is None else out + part
        out = out.astype(bf16)
        pa[zz] = out[:, :wa].reshape(XS, slots, wa)
        pb[zz] = out[:, wa:].reshape(XS, slots, width - wa)

    def sums_x(zd):
        zz = zat(zd)
        k, o, dev = passed_on(zd)
        send(pb.at[zz, xat(2)], cx_in.at[0, zz], cx_s.at[0, zz], cx_r.at[0, zz], (g, dev))
        send(pb.at[zz, xat(k)], cx_in.at[1, zz], cx_s.at[1, zz], cx_r.at[1, zz], (g, xr if k == 1 else xl))

    def sums_x_on(zd):
        zz = zat(zd)
        k, o, dev = passed_on(zd)
        arrived(cx_in.at[0, zz], cx_s.at[0, zz], cx_r.at[0, zz])
        cx_out[zz] = (cx_in[0, zz].astype(f32) + pb[zz, xat(o)].astype(f32)).astype(bf16)
        send(cx_out.at[zz], cx_in.at[2, zz], cx_s.at[2, zz], cx_r.at[2, zz], (g, dev))

    def forward_a(step, k):
        came_a(step, k)
        ring_a(step, k)

    def own_a(k):
        arrived(xa.at[z, xat(k)], a1_s.at[k], a1_r.at[xat(k)])
        ring_a(0, k)

    ring_b(0)
    for k in near:
        send(xa.at[z, x], xa.at[z, x], a1_s.at[k], a1_r.at[x], (g, inner_at(x + k, z)))
    ring_a(0, 0)
    spread_b(0)
    own_a(1)
    came_b(1)
    ring_b(1)
    spread_b(-1)
    spread_b(1)
    own_a(3)
    forward_a(1, 0)
    came_b(2)
    ring_b(2)
    spread_b(-2)
    spread_b(2)
    relay_b(0)
    own_a(2)
    forward_a(1, 1)
    came_b(3)
    ring_b(3)
    spread_b(-3)
    spread_b(3)
    forward_a(1, 3)
    forward_a(2, 0)
    relay_b(-1)
    relay_b(1)
    came_b(4)
    spread_b(4)
    for c in cw:
        c.wait()
    forward_a(1, 2)
    forward_a(2, 1)
    came_cols(0)
    compute(0)
    forward_a(2, 3)
    relay_b(-2)
    relay_b(2)
    forward_a(3, 0)
    forward_a(2, 2)
    for zd in (1, -1):
        came_cols(zd)
        compute(zd)
    sums_x(0)
    forward_a(3, 1)
    relay_b(-3)
    relay_b(3)
    forward_a(3, 3)
    forward_a(3, 2)
    for zd in (2, -2):
        came_cols(zd)
        compute(zd)
    relay_b(4)
    sums_x(1)
    sums_x(-1)
    for zd in (3, -3):
        came_cols(zd)
        compute(zd)
    sums_x_on(0)
    for k in (0, *near):
        came_a(4, k)
    came_cols(4)
    compute(4)

    order = (2, 1, 3, 0)
    first = (order[:2], order[2:])

    def start_ra(step, way, zd, dev, ks):
        for k in ks:
            send(pa.at[zat(zd), xat(k)], ra_buf.at[way, step, k], ra_s.at[way, step, k], ra_r.at[way, step, k], (g, dev))

    start_ra(0, 0, 4, right, first[0])
    start_ra(0, 1, 4, left, first[1])
    sums_x(4)
    start_ra(1, 0, 3, right, first[1])
    start_ra(1, 1, -3, left, first[0])
    for zd in (3, -3, 2, -2):
        sums_x(zd)
    sums_x_on(1)
    sums_x_on(-1)

    def came_ra(way, step, k):
        arrived(ra_buf.at[way, step - 1, k], ra_s.at[way, step - 1, k], ra_r.at[way, step - 1, k])
        return ra_buf[way, step - 1, k].astype(f32)

    def ring_ra(step, places=range(XS)):
        for j in places:
            for way, sgn, dev in ((0, 1, right), (1, -1, left)):
                k = (*first[1 - way], *first[way])[j]
                if step == 1 and k not in first[way]:
                    continue
                zz = zat(sgn * (4 - step))
                ra_buf[way, step - 1, k] = (came_ra(way, step, k) + pa[zz, xat(k)].astype(f32)).astype(bf16)
                send(ra_buf.at[way, step - 1, k], ra_buf.at[way, step, k], ra_s.at[way, step, k], ra_r.at[way, step, k], (g, dev))

    def col_sum(zz):
        for j in (1, 2):
            arrived(cx_in.at[j, zz], cx_s.at[j, zz], cx_r.at[j, zz])
        return pb[zz, x].astype(f32) + cx_in[1, zz].astype(f32) + cx_in[2, zz].astype(f32)

    def came_rb(way, step):
        dst = rb_buf.at[way, step]
        if step == 0:
            dst = dst.at[rows_of[way]]
        arrived(dst, rb_s.at[way, step], rb_r.at[way, step])

    def send_rb(way, step):
        src, dst = rb_out.at[way, step], rb_buf.at[way, step]
        if step == 0:
            src, dst = src.at[rows_of[way]], dst.at[rows_of[way]]
        send(src, dst, rb_s.at[way, step], rb_r.at[way, step], (g, (right, left)[way]))

    def start_rb():
        tot = col_sum(zat(4)).astype(bf16)
        for way in range(2):
            rb_out[way, 0] = tot
            send_rb(way, 0)

    def ring_rb(step):
        for way, sgn in ((0, 1), (1, -1)):
            tot = col_sum(zat(sgn * (4 - step)))
            came_rb(way, step - 1)
            if step == 1:
                rb_out[way, 1] = tot.astype(bf16)
                mine = slice(half * way, half * (way + 1))
                rb_out[way, 1, mine] = (tot[mine] + rb_buf[way, 0, mine].astype(f32)).astype(bf16)
            else:
                rb_out[way, step] = (tot + rb_buf[way, step - 1].astype(f32)).astype(bf16)
            send_rb(way, step)

    ring_ra(1)
    sums_x_on(4)
    ring_ra(2, (0, 1))
    sums_x_on(3)
    sums_x_on(-3)
    start_rb()
    ring_ra(2, (2, 3))
    sums_x_on(2)
    sums_x_on(-2)
    ring_rb(1)
    ring_ra(3, (0, 1))
    ring_rb(2)
    ring_ra(3, (2, 3))
    ring_rb(3)
    for k in order:
        rax_out[k] = (pa[z, xat(k)].astype(f32) + came_ra(0, 4, k) + came_ra(1, 4, k)).astype(bf16)
        if k:
            send(rax_out.at[k], rax_in.at[x], rax_s.at[k], rax_r.at[x], (g, inner_at(x + k, z)))

    def back(part, fin):
        for d in range(groups):
            ret_out[part][d] = fin[cap * d : cap * (d + 1)]

        @pl.loop(1, groups)
        def _(j):
            d = far_first(j)
            pltpu.make_async_remote_copy(
                src_ref=ret_out[part].at[d], dst_ref=ret_in[part].at[g], send_sem=ret_s.at[part, d],
                recv_sem=ret_r.at[part, g], device_id=(d, i), device_id_type=MESH,
            ).start()

        ret_in[part][g] = ret_out[part][g]

    tot = col_sum(z)
    for way in range(2):
        came_rb(way, 3)
        tot = tot + rb_buf[way, 3].astype(f32)
    back(1, tot.astype(bf16))
    tot = rax_out[0].astype(f32)
    for k in near:
        arrived(rax_in.at[xat(k)], rax_s.at[k], rax_r.at[xat(k)])
        tot = tot + rax_in[xat(k)].astype(f32)
    back(0, tot.astype(bf16))

    places_t = jnp.where(
        lax.broadcasted_iota(jnp.int32, (n_rows, slots), 1) == target_col, 1.0, 0.0
    ).astype(bf16)
    rw = jnp.sum(jnp.where(eye, rw_ref[...], 0.0), axis=1, keepdims=True)
    for part, columns in ((1, slice(wa, width)), (0, slice(0, wa))):

        @pl.loop(1, groups)
        def _(k):
            d = lax.rem(g + k, groups)
            arrived(ret_in[part].at[d], ret_s.at[part, d], ret_r.at[part, d])

        returned = jnp.concatenate([ret_in[part][d] for d in range(groups)], axis=0)
        combined = jnp.dot(places_t, returned, preferred_element_type=f32)
        o_ref[:, columns] = (combined * rw).astype(o_ref.dtype)

    for c in sent:
        c.wait_send()

    @pl.loop(1, groups)
    def _(k):
        d = lax.rem(g + k, groups)
        moved = [(out_buf, in_buf, a2a_s.at[d], a2a_r.at[g])]
        moved += [(ret_out[p], ret_in[p], ret_s.at[p, d], ret_r.at[p, g]) for p in range(2)]
        for src, dst, s, r in moved:
            pltpu.make_async_remote_copy(
                src_ref=src.at[d], dst_ref=dst.at[g], send_sem=s, recv_sem=r,
                device_id=(d, i), device_id_type=MESH,
            ).wait_send()


def body(pair_rows, group_ids, local_ids, route_weight, w_up, w_down):
    groups = lax.axis_size("group")
    n_rows, width = pair_rows.shape
    cap = 2 * n_rows // groups
    slots = groups * cap
    wa = 7 * width // 16
    wb = width - wa
    wide = width + TAG
    dma = pltpu.SemaphoreType.DMA
    vmem, hbm = pl.BlockSpec(memory_space=pltpu.VMEM), pl.BlockSpec(memory_space=pl.ANY)
    V = pltpu.VMEM
    scratch = [
        V(w_up.shape, bf16), V(w_down.shape, bf16), dma((2,)),
        V((groups, cap, wide), bf16), V((groups, cap, wide), bf16), dma((groups,)), dma((groups,)),
        V((ZS, XS, slots, wa), bf16), V((ZS, XS, slots, wb + TAG), bf16),
        dma((XS,)), dma((XS,)), dma((2, 4, XS)), dma((2, 4, XS)), dma((2, 4)), dma((2, 4)), dma((XS, ZS)), dma((XS, ZS)),
        V((ZS, XS, slots, wa), bf16), V((ZS, XS, slots, wb), bf16),
        dma((2, 4, XS)), dma((2, 4, XS)), V((2, 4, XS, slots, wa), bf16), dma((XS,)), dma((XS,)),
        V((XS, slots, wa), bf16), V((XS, slots, wa), bf16),
        dma((3, ZS)), dma((3, ZS)), V((3, ZS, slots, wb), bf16), V((ZS, slots, wb), bf16),
        dma((2, 4)), dma((2, 4)), V((2, 4, slots, wb), bf16), V((2, 4, slots, wb), bf16),
        [V((groups, cap, w), bf16) for w in (wa, wb)], [V((groups, cap, w), bf16) for w in (wa, wb)],
        dma((2, groups)), dma((2, groups)),
    ]
    return pl.pallas_call(
        kernel,
        out_shape=jax.ShapeDtypeStruct((n_rows, width), bf16),
        in_specs=[vmem] * 4 + [hbm] * 2,
        out_specs=vmem,
        scratch_shapes=scratch,
        compiler_params=pltpu.CompilerParams(
            collective_id=0, has_side_effects=True, vmem_limit_bytes=56 * 2**20
        ),
        name="routed_experts",
    )(
        pair_rows,
        group_ids.reshape(1, n_rows),
        local_ids.reshape(1, n_rows),
        route_weight.reshape(1, n_rows),
        w_up,
        w_down,
    )


def solution(mesh):
    placed = (
        P(("group", "inner"), None),
        P(("group", "inner"), None),
        P(("group", "inner"), None),
        P(("group", "inner")),
        P("group", None, "inner"),
        P("group", "inner", None),
    )
    return jax.shard_map(
        body, mesh=mesh, in_specs=placed, out_specs=P(("group", "inner"), None), check_vma=False
    )
```

```python
import functools

import jax
import jax.numpy as jnp
from jax import lax
from jax.experimental import pallas as pl
from jax.experimental.pallas import tpu as pltpu
from jax.sharding import PartitionSpec as P

MESH = pl.DeviceIdType.MESH
XS, ZS = 4, 8
TAG = 128
DIRECT = (4,)
f32, bf16 = jnp.float32, jnp.bfloat16


def kernel(
    rows_hbm, gid_hbm, lid_hbm, rw_hbm, wup_hbm, wdn_hbm, o_ref,
    rows_ref, gid_ref, lid_ref, rw_ref, isem, wup, wdn, wsem,
    out_buf, in_buf, a2a_s, a2a_r,
    xa, xb, a1_s, a1_r, a2_s, a2_r, b1_s, b1_r, b2_s, b2_r,
    pa, pb, ra_s, ra_r, ra_buf, rax_s, rax_r, rax_out, rax_in,
    cx_s, cx_r, cx_in, cx_out, rb_s, rb_r, rb_buf, rb_out,
    ret_out, ret_in, ret_s, ret_r,
):
    n_rows, width = rows_ref.shape
    groups, cap = out_buf.shape[0], out_buf.shape[1]
    slots = groups * cap
    half = slots // 2
    wa = xa.shape[-1]
    g = lax.axis_index("group")
    i = lax.axis_index("inner")
    x, z = i // ZS, i % ZS

    def inner_at(xx, zz):
        return lax.rem(xx + XS, XS) * ZS + lax.rem(zz + ZS, ZS)

    right, left = inner_at(x, z + 1), inner_at(x, z - 1)

    def zat(d):
        return lax.rem(z + d + ZS, ZS)

    def xat(k):
        return lax.rem(x + k, XS)

    sent = []

    def send(src, dst, s, r, dev):
        c = pltpu.make_async_remote_copy(
            src_ref=src, dst_ref=dst, send_sem=s, recv_sem=r, device_id=dev, device_id_type=MESH
        )
        c.start()
        sent.append(c)

    def arrived(dst, s, r):
        pltpu.make_async_remote_copy(
            src_ref=dst, dst_ref=dst, send_sem=s, recv_sem=r, device_id=(g, right), device_id_type=MESH
        ).wait_recv()

    barrier = pltpu.get_barrier_semaphore()

    def far_first(j):
        return lax.rem(g + groups // 2 + (2 * lax.rem(j, 2) - 1) * (j // 2), groups)

    @pl.loop(1, groups)
    def _(j):
        pl.semaphore_signal(barrier, inc=1, device_id=(far_first(j), i), device_id_type=MESH)

    for k in range(1, XS):
        pl.semaphore_signal(barrier, inc=1, device_id=(g, inner_at(x + k, z)), device_id_type=MESH)
    for dev in (right, left):
        pl.semaphore_signal(barrier, inc=1, device_id=(g, dev), device_id_type=MESH)

    cin = [
        pltpu.make_async_copy(src, dst, isem.at[n])
        for n, (src, dst) in enumerate(
            ((gid_hbm, gid_ref), (lid_hbm, lid_ref), (rw_hbm, rw_ref), (rows_hbm, rows_ref))
        )
    ]
    for c in cin:
        c.start()
    cw = [
        pltpu.make_async_copy(wup_hbm, wup, wsem.at[0]),
        pltpu.make_async_copy(wdn_hbm, wdn, wsem.at[1]),
    ]
    for c in cw:
        c.start()

    for c in cin:
        c.wait()

    gid = gid_ref[...]
    sub = lax.broadcasted_iota(jnp.int32, (n_rows, n_rows), 0)
    lane = lax.broadcasted_iota(jnp.int32, (n_rows, n_rows), 1)
    eye = sub == lane
    gcol = jnp.sum(jnp.where(eye, gid, 0), axis=1, keepdims=True)
    before_row = jnp.where((gcol == gid) & (sub < lane), 1, 0)
    target = gid * cap + jnp.sum(before_row, axis=0, keepdims=True)
    target_col = jnp.sum(jnp.where(eye, target, 0), axis=1, keepdims=True)
    places = lax.broadcasted_iota(jnp.int32, (slots, n_rows), 0) == target
    out_rows = jnp.dot(
        jnp.where(places, 1.0, 0.0).astype(bf16), rows_ref[...], preferred_element_type=f32
    ).astype(bf16)
    tags = jnp.sum(jnp.where(places, lid_ref[...], 0), axis=1, keepdims=True).astype(f32)
    out_tags = jnp.broadcast_to(tags, (slots, TAG)).astype(bf16)
    for d in range(groups):
        out_buf[d, :, :width] = out_rows[cap * d : cap * (d + 1)]
        out_buf[d, :, width:] = out_tags[cap * d : cap * (d + 1)]

    pl.semaphore_wait(barrier, groups - 1 + XS - 1 + 2)

    @pl.loop(1, groups)
    def _(j):
        d = far_first(j)
        pltpu.make_async_remote_copy(
            src_ref=out_buf.at[d], dst_ref=in_buf.at[g], send_sem=a2a_s.at[d], recv_sem=a2a_r.at[g],
            device_id=(d, i), device_id_type=MESH,
        ).start()

    in_buf[g] = out_buf[g]

    @pl.loop(1, groups)
    def _(k):
        d = lax.rem(g + k, groups)
        arrived(in_buf.at[d], a2a_s.at[d], a2a_r.at[d])

    for d in range(groups):
        xa[z, x, cap * d : cap * (d + 1), :] = in_buf[d, :, :wa]
        xb[z, x, cap * d : cap * (d + 1), :] = in_buf[d, :, wa:]

    near = (1, 3, 2)
    last = ((0, 1), (3, 2))
    xr, xl = inner_at(x + 1, z), inner_at(x - 1, z)
    rows_of = (pl.ds(0, half), pl.ds(half, half))
    ways = ((0, -1, right), (1, 1, left))

    def passed_on(zd):
        return (3, 1, xr) if zd in (0, -1, -2, -3) else (1, 3, xl)

    def spread_b(zd):
        blk = xb.at[zat(zd), x]
        send(blk, blk, b2_s.at[1, zat(zd)], b2_r.at[x, zat(zd)], (g, xr))
        send(blk, blk, b2_s.at[3, zat(zd)], b2_r.at[x, zat(zd)], (g, xl))
        if zd in DIRECT:
            send(blk, blk, b2_s.at[2, zat(zd)], b2_r.at[x, zat(zd)], (g, inner_at(x + 2, z)))

    def came_col(zd, k):
        arrived(xb.at[zat(zd), xat(k)], b2_s.at[2, zat(zd)], b2_r.at[xat(k), zat(zd)])

    def relay_b(zd):
        if zd in DIRECT:
            return
        k, _, dev = passed_on(zd)
        came_col(zd, k)
        blk = xb.at[zat(zd), xat(k)]
        send(blk, blk, b2_s.at[2, zat(zd)], b2_r.at[xat(k), zat(zd)], (g, dev))

    def came_cols(zd):
        if zd in DIRECT:
            came_col(zd, passed_on(zd)[0])
        came_col(zd, passed_on(zd)[1])
        came_col(zd, 2)

    def ring_b(step):
        for way, sgn, dev in ways:
            blk = xb.at[zat(sgn * step), x]
            if step == 3:
                blk = blk.at[rows_of[way]]
            send(blk, blk, b1_s.at[way, step], b1_r.at[way, step], (g, dev))

    def came_b(step):
        for way, sgn, _ in ways:
            blk = xb.at[zat(sgn * step), x]
            if step == 4:
                blk = blk.at[rows_of[way]]
            arrived(blk, b1_s.at[way, step - 1], b1_r.at[way, step - 1])

    def ring_a(step, k):
        for way, sgn, dev in ways:
            if step < 3 or k in last[way]:
                blk = xa.at[zat(sgn * step), xat(k)]
                send(blk, blk, a2_s.at[way, step, k], a2_r.at[way, step, k], (g, dev))

    def came_a(step, k):
        for way, sgn, _ in ways:
            if step < 4 or k in last[way]:
                arrived(xa.at[zat(sgn * step), xat(k)], a2_s.at[way, step - 1, k], a2_r.at[way, step - 1, k])

    def compute(zd):
        zz = zat(zd)
        va = xa[zz].reshape(XS * slots, wa)
        vb = xb[zz].reshape(XS * slots, width - wa + TAG)
        tag = vb[:, width - wa :].astype(f32)
        out = None
        for e in range(2):
            up = jnp.dot(va, wup[e, :wa], preferred_element_type=f32)
            up = up + jnp.dot(vb[:, : width - wa], wup[e, wa:], preferred_element_type=f32)
            hid = up / (1.0 + jnp.exp(-up))
            mask = jnp.where(tag == float(e), 1.0, 0.0)
            hid = (hid * jnp.concatenate([mask] * (hid.shape[1] // TAG), axis=1)).astype(bf16)
            part = jnp.dot(hid, wdn[e], preferred_element_type=f32)
            out = part if out is None else out + part
        out = out.astype(bf16)
        pa[zz] = out[:, :wa].reshape(XS, slots, wa)
        pb[zz] = out[:, wa:].reshape(XS, slots, width - wa)

    def sums_x(zd):
        zz = zat(zd)
        if zd in DIRECT:
            for k in near:
                send(pb.at[zz, xat(k)], cx_in.at[k - 1, zz], cx_s.at[k - 1, zz], cx_r.at[k - 1, zz], (g, inner_at(x + k, z)))
            return
        k, o, dev = passed_on(zd)
        send(pb.at[zz, xat(2)], cx_in.at[0, zz], cx_s.at[0, zz], cx_r.at[0, zz], (g, dev))
        send(pb.at[zz, xat(k)], cx_in.at[1, zz], cx_s.at[1, zz], cx_r.at[1, zz], (g, xr if k == 1 else xl))

    def sums_x_on(zd):
        if zd in DIRECT:
            return
        zz = zat(zd)
        k, o, dev = passed_on(zd)
        arrived(cx_in.at[0, zz], cx_s.at[0, zz], cx_r.at[0, zz])
        cx_out[zz] = (cx_in[0, zz].astype(f32) + pb[zz, xat(o)].astype(f32)).astype(bf16)
        send(cx_out.at[zz], cx_in.at[2, zz], cx_s.at[2, zz], cx_r.at[2, zz], (g, dev))

    def forward_a(step, k):
        came_a(step, k)
        ring_a(step, k)

    def own_a(k):
        arrived(xa.at[z, xat(k)], a1_s.at[k], a1_r.at[xat(k)])
        ring_a(0, k)

    ring_b(0)
    for k in near:
        send(xa.at[z, x], xa.at[z, x], a1_s.at[k], a1_r.at[x], (g, inner_at(x + k, z)))
    ring_a(0, 0)
    spread_b(0)
    own_a(1)
    came_b(1)
    ring_b(1)
    spread_b(-1)
    spread_b(1)
    own_a(3)
    forward_a(1, 0)
    came_b(2)
    ring_b(2)
    spread_b(-2)
    spread_b(2)
    relay_b(0)
    own_a(2)
    forward_a(1, 1)
    came_b(3)
    ring_b(3)
    spread_b(-3)
    spread_b(3)
    forward_a(1, 3)
    forward_a(2, 0)
    relay_b(-1)
    relay_b(1)
    came_b(4)
    spread_b(4)
    for c in cw:
        c.wait()
    forward_a(1, 2)
    forward_a(2, 1)
    came_cols(0)
    compute(0)
    forward_a(2, 3)
    relay_b(-2)
    relay_b(2)
    forward_a(3, 0)
    forward_a(2, 2)
    for zd in (1, -1):
        came_cols(zd)
        compute(zd)
    sums_x(0)
    forward_a(3, 1)
    relay_b(-3)
    relay_b(3)
    forward_a(3, 3)
    forward_a(3, 2)
    for zd in (2, -2):
        came_cols(zd)
        compute(zd)
    for zd in (3, -3):
        came_cols(zd)
        compute(zd)
    sums_x_on(0)
    for k in (0, *near):
        came_a(4, k)
    came_cols(4)
    compute(4)

    order = (2, 1, 3, 0)
    first = (order[:2], order[2:])

    def start_ra(step, way, zd, dev, ks):
        for k in ks:
            send(pa.at[zat(zd), xat(k)], ra_buf.at[way, step, k], ra_s.at[way, step, k], ra_r.at[way, step, k], (g, dev))

    sums_x(4)
    start_ra(0, 0, 4, right, first[0])
    start_ra(0, 1, 4, left, first[1])
    sums_x(3)
    start_ra(1, 0, 3, right, first[1])
    start_ra(1, 1, -3, left, first[0])

    def came_ra(way, step, k):
        arrived(ra_buf.at[way, step - 1, k], ra_s.at[way, step - 1, k], ra_r.at[way, step - 1, k])
        return ra_buf[way, step - 1, k].astype(f32)

    def ring_ra(step, places=range(XS)):
        for j in places:
            for way, sgn, dev in ((0, 1, right), (1, -1, left)):
                k = (*first[1 - way], *first[way])[j]
                if step == 1 and k not in first[way]:
                    continue
                zz = zat(sgn * (4 - step))
                ra_buf[way, step - 1, k] = (came_ra(way, step, k) + pa[zz, xat(k)].astype(f32)).astype(bf16)
                send(ra_buf.at[way, step - 1, k], ra_buf.at[way, step, k], ra_s.at[way, step, k], ra_r.at[way, step, k], (g, dev))

    def col_sum(zd):
        zz = zat(zd)
        tot = pb[zz, x].astype(f32)
        for j in (0, 1, 2) if zd in DIRECT else (1, 2):
            arrived(cx_in.at[j, zz], cx_s.at[j, zz], cx_r.at[j, zz])
            tot = tot + cx_in[j, zz].astype(f32)
        return tot

    def came_rb(way, step):
        dst = rb_buf.at[way, step]
        if step == 0:
            dst = dst.at[rows_of[way]]
        arrived(dst, rb_s.at[way, step], rb_r.at[way, step])

    def send_rb(way, step):
        src, dst = rb_out.at[way, step], rb_buf.at[way, step]
        if step == 0:
            src, dst = src.at[rows_of[way]], dst.at[rows_of[way]]
        send(src, dst, rb_s.at[way, step], rb_r.at[way, step], (g, (right, left)[way]))

    def start_rb():
        tot = col_sum(4).astype(bf16)
        for way in range(2):
            rb_out[way, 0] = tot
            send_rb(way, 0)

    def ring_rb(step):
        for way, sgn in ((0, 1), (1, -1)):
            tot = col_sum(sgn * (4 - step))
            came_rb(way, step - 1)
            if step == 1:
                rb_out[way, 1] = tot.astype(bf16)
                mine = slice(half * way, half * (way + 1))
                rb_out[way, 1, mine] = (tot[mine] + rb_buf[way, 0, mine].astype(f32)).astype(bf16)
            else:
                rb_out[way, step] = (tot + rb_buf[way, step - 1].astype(f32)).astype(bf16)
            send_rb(way, step)

    sums_x(-3)
    ring_ra(1)
    sums_x_on(3)
    start_rb()
    sums_x(2)
    ring_ra(2, (0, 1))
    sums_x_on(-3)
    sums_x(-2)
    ring_rb(1)
    ring_ra(2, (2, 3))
    sums_x_on(2)
    sums_x(1)
    sums_x_on(-2)
    sums_x(-1)
    ring_rb(2)
    ring_ra(3, (0, 1))
    sums_x_on(1)
    sums_x_on(-1)
    ring_ra(3, (2, 3))
    ring_rb(3)
    for k in order:
        rax_out[k] = (pa[z, xat(k)].astype(f32) + came_ra(0, 4, k) + came_ra(1, 4, k)).astype(bf16)
        if k:
            send(rax_out.at[k], rax_in.at[x], rax_s.at[k], rax_r.at[x], (g, inner_at(x + k, z)))

    def back(part, fin):
        for d in range(groups):
            ret_out[part][d] = fin[cap * d : cap * (d + 1)]

        @pl.loop(1, groups)
        def _(j):
            d = far_first(j)
            pltpu.make_async_remote_copy(
                src_ref=ret_out[part].at[d], dst_ref=ret_in[part].at[g], send_sem=ret_s.at[part, d],
                recv_sem=ret_r.at[part, g], device_id=(d, i), device_id_type=MESH,
            ).start()

        ret_in[part][g] = ret_out[part][g]

    tot = col_sum(0)
    for way in range(2):
        came_rb(way, 3)
        tot = tot + rb_buf[way, 3].astype(f32)
    back(1, tot.astype(bf16))
    tot = rax_out[0].astype(f32)
    for k in near:
        arrived(rax_in.at[xat(k)], rax_s.at[k], rax_r.at[xat(k)])
        tot = tot + rax_in[xat(k)].astype(f32)
    back(0, tot.astype(bf16))

    for c in sent:
        c.wait_send()

    @pl.loop(1, groups)
    def _(k):
        d = lax.rem(g + k, groups)
        moved = [(out_buf, in_buf, a2a_s.at[d], a2a_r.at[g])]
        moved += [(ret_out[p], ret_in[p], ret_s.at[p, d], ret_r.at[p, g]) for p in range(2)]
        for src, dst, s, r in moved:
            pltpu.make_async_remote_copy(
                src_ref=src.at[d], dst_ref=dst.at[g], send_sem=s, recv_sem=r,
                device_id=(d, i), device_id_type=MESH,
            ).wait_send()

    places_t = jnp.where(
        lax.broadcasted_iota(jnp.int32, (n_rows, slots), 1) == target_col, 1.0, 0.0
    ).astype(bf16)
    rw = jnp.sum(jnp.where(eye, rw_ref[...], 0.0), axis=1, keepdims=True)
    for part, columns in ((1, slice(wa, width)), (0, slice(0, wa))):

        @pl.loop(1, groups)
        def _(k):
            d = lax.rem(g + k, groups)
            arrived(ret_in[part].at[d], ret_s.at[part, d], ret_r.at[part, d])

        returned = jnp.concatenate([ret_in[part][d] for d in range(groups)], axis=0)
        combined = jnp.dot(places_t, returned, preferred_element_type=f32)
        o_ref[:, columns] = (combined * rw).astype(o_ref.dtype)


def body(pair_rows, group_ids, local_ids, route_weight, w_up, w_down):
    groups = lax.axis_size("group")
    n_rows, width = pair_rows.shape
    cap = 2 * n_rows // groups
    slots = groups * cap
    wa = 8 * width // 16
    wb = width - wa
    wide = width + TAG
    dma = pltpu.SemaphoreType.DMA
    vmem, hbm = pl.BlockSpec(memory_space=pltpu.VMEM), pl.BlockSpec(memory_space=pl.ANY)
    V = pltpu.VMEM
    scratch = [
        V((n_rows, width), bf16), V((1, n_rows), jnp.int32), V((1, n_rows), jnp.int32), V((1, n_rows), f32), dma((4,)),
        V(w_up.shape, bf16), V(w_down.shape, bf16), dma((2,)),
        V((groups, cap, wide), bf16), V((groups, cap, wide), bf16), dma((groups,)), dma((groups,)),
        V((ZS, XS, slots, wa), bf16), V((ZS, XS, slots, wb + TAG), bf16),
        dma((XS,)), dma((XS,)), dma((2, 4, XS)), dma((2, 4, XS)), dma((2, 4)), dma((2, 4)), dma((XS, ZS)), dma((XS, ZS)),
        V((ZS, XS, slots, wa), bf16), V((ZS, XS, slots, wb), bf16),
        dma((2, 4, XS)), dma((2, 4, XS)), V((2, 4, XS, slots, wa), bf16), dma((XS,)), dma((XS,)),
        V((XS, slots, wa), bf16), V((XS, slots, wa), bf16),
        dma((3, ZS)), dma((3, ZS)), V((3, ZS, slots, wb), bf16), V((ZS, slots, wb), bf16),
        dma((2, 4)), dma((2, 4)), V((2, 4, slots, wb), bf16), V((2, 4, slots, wb), bf16),
        [V((groups, cap, w), bf16) for w in (wa, wb)], [V((groups, cap, w), bf16) for w in (wa, wb)],
        dma((2, groups)), dma((2, groups)),
    ]
    return pl.pallas_call(
        kernel,
        out_shape=jax.ShapeDtypeStruct((n_rows, width), bf16),
        in_specs=[hbm] * 6,
        out_specs=vmem,
        scratch_shapes=scratch,
        compiler_params=pltpu.CompilerParams(
            collective_id=0, has_side_effects=True, vmem_limit_bytes=56 * 2**20
        ),
        name="routed_experts",
    )(
        pair_rows,
        group_ids.reshape(1, n_rows),
        local_ids.reshape(1, n_rows),
        route_weight.reshape(1, n_rows),
        w_up,
        w_down,
    )


def solution(mesh):
    placed = (
        P(("group", "inner"), None),
        P(("group", "inner"), None),
        P(("group", "inner"), None),
        P(("group", "inner")),
        P("group", None, "inner"),
        P("group", "inner", None),
    )
    return jax.shard_map(
        body, mesh=mesh, in_specs=placed, out_specs=P(("group", "inner"), None), check_vma=False
    )
```

```python
import functools

import jax
import jax.numpy as jnp
from jax import lax
from jax.experimental import pallas as pl
from jax.experimental.pallas import tpu as pltpu
from jax.sharding import PartitionSpec as P

MESH = pl.DeviceIdType.MESH
XS, ZS = 4, 8
TAG = 128
DIRECT = (4,)
f32, bf16 = jnp.float32, jnp.bfloat16


def kernel(
    rows_hbm, gid_hbm, lid_hbm, rw_hbm, wup_hbm, wdn_hbm, o_ref,
    rows_ref, gid_ref, lid_ref, rw_ref, isem, wup, wdn, wsem,
    out_buf, in_buf, a2a_s, a2a_r,
    xa, xb, a1_s, a1_r, a2_s, a2_r, b1_s, b1_r, b2_s, b2_r,
    pa, pb, ra_s, ra_r, ra_buf, rax_s, rax_r, rax_out, rax_in,
    cx_s, cx_r, cx_in, cx_out, rb_s, rb_r, rb_buf, rb_out,
    ret_out, ret_in, ret_s, ret_r,
):
    n_rows, width = rows_ref.shape
    groups, cap = out_buf.shape[0], out_buf.shape[1]
    slots = groups * cap
    half = slots // 2
    wa = xa.shape[-1]
    g = lax.axis_index("group")
    i = lax.axis_index("inner")
    x, z = i // ZS, i % ZS

    def inner_at(xx, zz):
        return lax.rem(xx + XS, XS) * ZS + lax.rem(zz + ZS, ZS)

    right, left = inner_at(x, z + 1), inner_at(x, z - 1)

    def zat(d):
        return lax.rem(z + d + ZS, ZS)

    def xat(k):
        return lax.rem(x + k, XS)

    sent = []

    def send(src, dst, s, r, dev):
        c = pltpu.make_async_remote_copy(
            src_ref=src, dst_ref=dst, send_sem=s, recv_sem=r, device_id=dev, device_id_type=MESH
        )
        c.start()
        sent.append(c)

    def arrived(dst, s, r):
        pltpu.make_async_remote_copy(
            src_ref=dst, dst_ref=dst, send_sem=s, recv_sem=r, device_id=(g, right), device_id_type=MESH
        ).wait_recv()

    barrier = pltpu.get_barrier_semaphore()

    def far_first(j):
        return lax.rem(g + groups // 2 + (2 * lax.rem(j, 2) - 1) * (j // 2), groups)

    @pl.loop(1, groups)
    def _(j):
        pl.semaphore_signal(barrier, inc=1, device_id=(far_first(j), i), device_id_type=MESH)

    for k in range(1, XS):
        pl.semaphore_signal(barrier, inc=1, device_id=(g, inner_at(x + k, z)), device_id_type=MESH)
    for dev in (right, left):
        pl.semaphore_signal(barrier, inc=1, device_id=(g, dev), device_id_type=MESH)

    cin = [
        pltpu.make_async_copy(src, dst, isem.at[n])
        for n, (src, dst) in enumerate(
            ((gid_hbm, gid_ref), (lid_hbm, lid_ref), (rw_hbm, rw_ref), (rows_hbm, rows_ref))
        )
    ]
    for c in cin:
        c.start()
    cw = [
        pltpu.make_async_copy(wup_hbm, wup, wsem.at[0]),
        pltpu.make_async_copy(wdn_hbm, wdn, wsem.at[1]),
    ]
    for c in cw:
        c.start()

    for c in cin:
        c.wait()

    gid = gid_ref[...]
    sub = lax.broadcasted_iota(jnp.int32, (n_rows, n_rows), 0)
    lane = lax.broadcasted_iota(jnp.int32, (n_rows, n_rows), 1)
    eye = sub == lane
    gcol = jnp.sum(jnp.where(eye, gid, 0), axis=1, keepdims=True)
    before_row = jnp.where((gcol == gid) & (sub < lane), 1, 0)
    target = gid * cap + jnp.sum(before_row, axis=0, keepdims=True)
    target_col = jnp.sum(jnp.where(eye, target, 0), axis=1, keepdims=True)
    places = lax.broadcasted_iota(jnp.int32, (slots, n_rows), 0) == target
    out_rows = jnp.dot(
        jnp.where(places, 1.0, 0.0).astype(bf16), rows_ref[...], preferred_element_type=f32
    ).astype(bf16)
    tags = jnp.sum(jnp.where(places, lid_ref[...], 0), axis=1, keepdims=True).astype(f32)
    out_tags = jnp.broadcast_to(tags, (slots, TAG)).astype(bf16)
    for d in range(groups):
        out_buf[d, :, :width] = out_rows[cap * d : cap * (d + 1)]
        out_buf[d, :, width:] = out_tags[cap * d : cap * (d + 1)]

    pl.semaphore_wait(barrier, groups - 1 + XS - 1 + 2)

    @pl.loop(1, groups)
    def _(j):
        d = far_first(j)
        pltpu.make_async_remote_copy(
            src_ref=out_buf.at[d], dst_ref=in_buf.at[g], send_sem=a2a_s.at[d], recv_sem=a2a_r.at[g],
            device_id=(d, i), device_id_type=MESH,
        ).start()

    in_buf[g] = out_buf[g]

    @pl.loop(1, groups)
    def _(k):
        d = lax.rem(g + k, groups)
        arrived(in_buf.at[d], a2a_s.at[d], a2a_r.at[d])

    for d in range(groups):
        xa[z, x, cap * d : cap * (d + 1), :] = in_buf[d, :, :wa]
        xb[z, x, cap * d : cap * (d + 1), :] = in_buf[d, :, wa:]

    near = (1, 3, 2)
    last = ((0, 1), (3, 2))
    xr, xl = inner_at(x + 1, z), inner_at(x - 1, z)
    rows_of = (pl.ds(0, half), pl.ds(half, half))
    ways = ((0, -1, right), (1, 1, left))

    def passed_on(zd):
        return (3, 1, xr) if zd in (0, -1, -2, -3) else (1, 3, xl)

    def spread_b(zd):
        blk = xb.at[zat(zd), x]
        send(blk, blk, b2_s.at[1, zat(zd)], b2_r.at[x, zat(zd)], (g, xr))
        send(blk, blk, b2_s.at[3, zat(zd)], b2_r.at[x, zat(zd)], (g, xl))
        if zd in DIRECT:
            send(blk, blk, b2_s.at[2, zat(zd)], b2_r.at[x, zat(zd)], (g, inner_at(x + 2, z)))

    def came_col(zd, k):
        arrived(xb.at[zat(zd), xat(k)], b2_s.at[2, zat(zd)], b2_r.at[xat(k), zat(zd)])

    def relay_b(zd):
        if zd in DIRECT:
            return
        k, _, dev = passed_on(zd)
        came_col(zd, k)
        blk = xb.at[zat(zd), xat(k)]
        send(blk, blk, b2_s.at[2, zat(zd)], b2_r.at[xat(k), zat(zd)], (g, dev))

    def came_cols(zd):
        if zd in DIRECT:
            came_col(zd, passed_on(zd)[0])
        came_col(zd, passed_on(zd)[1])
        came_col(zd, 2)

    def ring_b(step):
        for way, sgn, dev in ways:
            blk = xb.at[zat(sgn * step), x]
            if step == 3:
                blk = blk.at[rows_of[way]]
            send(blk, blk, b1_s.at[way, step], b1_r.at[way, step], (g, dev))

    def came_b(step):
        for way, sgn, _ in ways:
            blk = xb.at[zat(sgn * step), x]
            if step == 4:
                blk = blk.at[rows_of[way]]
            arrived(blk, b1_s.at[way, step - 1], b1_r.at[way, step - 1])

    def ring_a(step, k):
        for way, sgn, dev in ways:
            if step < 3 or k in last[way]:
                blk = xa.at[zat(sgn * step), xat(k)]
                send(blk, blk, a2_s.at[way, step, k], a2_r.at[way, step, k], (g, dev))

    def came_a(step, k):
        for way, sgn, _ in ways:
            if step < 4 or k in last[way]:
                arrived(xa.at[zat(sgn * step), xat(k)], a2_s.at[way, step - 1, k], a2_r.at[way, step - 1, k])

    def compute(zd):
        zz = zat(zd)
        va = xa[zz].reshape(XS * slots, wa)
        vb = xb[zz].reshape(XS * slots, width - wa + TAG)
        tag = vb[:, width - wa :].astype(f32)
        out = None
        for e in range(2):
            up = jnp.dot(va, wup[e, :wa], preferred_element_type=f32)
            up = up + jnp.dot(vb[:, : width - wa], wup[e, wa:], preferred_element_type=f32)
            hid = up / (1.0 + jnp.exp(-up))
            mask = jnp.where(tag == float(e), 1.0, 0.0)
            hid = (hid * jnp.concatenate([mask] * (hid.shape[1] // TAG), axis=1)).astype(bf16)
            part = jnp.dot(hid, wdn[e], preferred_element_type=f32)
            out = part if out is None else out + part
        out = out.astype(bf16)
        pa[zz] = out[:, :wa].reshape(XS, slots, wa)
        pb[zz] = out[:, wa:].reshape(XS, slots, width - wa)

    def sums_x(zd):
        zz = zat(zd)
        if zd in DIRECT:
            for k in near:
                send(pb.at[zz, xat(k)], cx_in.at[k - 1, zz], cx_s.at[k - 1, zz], cx_r.at[k - 1, zz], (g, inner_at(x + k, z)))
            return
        k, o, dev = passed_on(zd)
        send(pb.at[zz, xat(2)], cx_in.at[0, zz], cx_s.at[0, zz], cx_r.at[0, zz], (g, dev))
        send(pb.at[zz, xat(k)], cx_in.at[1, zz], cx_s.at[1, zz], cx_r.at[1, zz], (g, xr if k == 1 else xl))

    def sums_x_on(zd):
        if zd in DIRECT:
            return
        zz = zat(zd)
        k, o, dev = passed_on(zd)
        arrived(cx_in.at[0, zz], cx_s.at[0, zz], cx_r.at[0, zz])
        cx_out[zz] = (cx_in[0, zz].astype(f32) + pb[zz, xat(o)].astype(f32)).astype(bf16)
        send(cx_out.at[zz], cx_in.at[2, zz], cx_s.at[2, zz], cx_r.at[2, zz], (g, dev))

    def forward_a(step, k):
        came_a(step, k)
        ring_a(step, k)

    def own_a(k):
        arrived(xa.at[z, xat(k)], a1_s.at[k], a1_r.at[xat(k)])
        ring_a(0, k)

    ring_b(0)
    for k in near:
        send(xa.at[z, x], xa.at[z, x], a1_s.at[k], a1_r.at[x], (g, inner_at(x + k, z)))
    ring_a(0, 0)
    spread_b(0)
    own_a(1)
    came_b(1)
    ring_b(1)
    spread_b(-1)
    spread_b(1)
    own_a(3)
    forward_a(1, 0)
    came_b(2)
    ring_b(2)
    spread_b(-2)
    spread_b(2)
    relay_b(0)
    own_a(2)
    forward_a(1, 1)
    came_b(3)
    ring_b(3)
    spread_b(-3)
    spread_b(3)
    forward_a(1, 3)
    forward_a(2, 0)
    relay_b(-1)
    relay_b(1)
    came_b(4)
    spread_b(4)
    for c in cw:
        c.wait()
    forward_a(1, 2)
    forward_a(2, 1)
    came_cols(0)
    compute(0)
    forward_a(2, 3)
    relay_b(-2)
    relay_b(2)
    forward_a(3, 0)
    forward_a(2, 2)
    came_cols(1)
    compute(1)
    forward_a(3, 1)
    came_cols(-1)
    compute(-1)
    sums_x(0)
    relay_b(-3)
    relay_b(3)
    forward_a(3, 3)
    came_cols(2)
    compute(2)
    forward_a(3, 2)
    came_cols(-2)
    compute(-2)
    for zd in (3, -3):
        came_cols(zd)
        compute(zd)
    sums_x_on(0)
    for k in (0, *near):
        came_a(4, k)
    came_cols(4)
    compute(4)

    order = (2, 1, 3, 0)
    first = (order[:2], order[2:])

    def start_ra(step, way, zd, dev, ks):
        for k in ks:
            send(pa.at[zat(zd), xat(k)], ra_buf.at[way, step, k], ra_s.at[way, step, k], ra_r.at[way, step, k], (g, dev))

    sums_x(4)
    start_ra(0, 0, 4, right, first[0])
    start_ra(0, 1, 4, left, first[1])
    sums_x(3)
    start_ra(1, 0, 3, right, first[1])
    start_ra(1, 1, -3, left, first[0])

    def came_ra(way, step, k):
        arrived(ra_buf.at[way, step - 1, k], ra_s.at[way, step - 1, k], ra_r.at[way, step - 1, k])
        return ra_buf[way, step - 1, k].astype(f32)

    def ring_ra(step, places=range(XS)):
        for j in places:
            for way, sgn, dev in ((0, 1, right), (1, -1, left)):
                k = (*first[1 - way], *first[way])[j]
                if step == 1 and k not in first[way]:
                    continue
                zz = zat(sgn * (4 - step))
                ra_buf[way, step - 1, k] = (came_ra(way, step, k) + pa[zz, xat(k)].astype(f32)).astype(bf16)
                send(ra_buf.at[way, step - 1, k], ra_buf.at[way, step, k], ra_s.at[way, step, k], ra_r.at[way, step, k], (g, dev))

    def col_sum(zd):
        zz = zat(zd)
        tot = pb[zz, x].astype(f32)
        for j in (0, 1, 2) if zd in DIRECT else (1, 2):
            arrived(cx_in.at[j, zz], cx_s.at[j, zz], cx_r.at[j, zz])
            tot = tot + cx_in[j, zz].astype(f32)
        return tot

    def came_rb(way, step):
        dst = rb_buf.at[way, step]
        if step == 0:
            dst = dst.at[rows_of[way]]
        arrived(dst, rb_s.at[way, step], rb_r.at[way, step])

    def send_rb(way, step):
        src, dst = rb_out.at[way, step], rb_buf.at[way, step]
        if step == 0:
            src, dst = src.at[rows_of[way]], dst.at[rows_of[way]]
        send(src, dst, rb_s.at[way, step], rb_r.at[way, step], (g, (right, left)[way]))

    def start_rb():
        tot = col_sum(4).astype(bf16)
        for way in range(2):
            rb_out[way, 0] = tot
            send_rb(way, 0)

    def ring_rb(step):
        for way, sgn in ((0, 1), (1, -1)):
            tot = col_sum(sgn * (4 - step))
            came_rb(way, step - 1)
            if step == 1:
                rb_out[way, 1] = tot.astype(bf16)
                mine = slice(half * way, half * (way + 1))
                rb_out[way, 1, mine] = (tot[mine] + rb_buf[way, 0, mine].astype(f32)).astype(bf16)
            else:
                rb_out[way, step] = (tot + rb_buf[way, step - 1].astype(f32)).astype(bf16)
            send_rb(way, step)

    sums_x(-3)
    ring_ra(1)
    sums_x_on(3)
    start_rb()
    sums_x(2)
    ring_ra(2, (0, 1))
    sums_x_on(-3)
    sums_x(-2)
    ring_rb(1)
    ring_ra(2, (2, 3))
    sums_x_on(2)
    sums_x(1)
    sums_x_on(-2)
    sums_x(-1)
    ring_rb(2)
    ring_ra(3, (0, 1))
    sums_x_on(1)
    sums_x_on(-1)
    ring_ra(3, (2, 3))
    ring_rb(3)
    for k in order:
        rax_out[k] = (pa[z, xat(k)].astype(f32) + came_ra(0, 4, k) + came_ra(1, 4, k)).astype(bf16)
        if k:
            send(rax_out.at[k], rax_in.at[x], rax_s.at[k], rax_r.at[x], (g, inner_at(x + k, z)))

    def back(part, fin):
        for d in range(groups):
            ret_out[part][d] = fin[cap * d : cap * (d + 1)]

        @pl.loop(1, groups)
        def _(j):
            d = far_first(j)
            pltpu.make_async_remote_copy(
                src_ref=ret_out[part].at[d], dst_ref=ret_in[part].at[g], send_sem=ret_s.at[part, d],
                recv_sem=ret_r.at[part, g], device_id=(d, i), device_id_type=MESH,
            ).start()

        ret_in[part][g] = ret_out[part][g]

    tot = col_sum(0)
    for way in range(2):
        came_rb(way, 3)
        tot = tot + rb_buf[way, 3].astype(f32)
    back(1, tot.astype(bf16))
    tot = rax_out[0].astype(f32)
    for k in near:
        arrived(rax_in.at[xat(k)], rax_s.at[k], rax_r.at[xat(k)])
        tot = tot + rax_in[xat(k)].astype(f32)
    back(0, tot.astype(bf16))

    for c in sent:
        c.wait_send()

    @pl.loop(1, groups)
    def _(k):
        d = lax.rem(g + k, groups)
        moved = [(out_buf, in_buf, a2a_s.at[d], a2a_r.at[g])]
        moved += [(ret_out[p], ret_in[p], ret_s.at[p, d], ret_r.at[p, g]) for p in range(2)]
        for src, dst, s, r in moved:
            pltpu.make_async_remote_copy(
                src_ref=src.at[d], dst_ref=dst.at[g], send_sem=s, recv_sem=r,
                device_id=(d, i), device_id_type=MESH,
            ).wait_send()

    places_t = jnp.where(
        lax.broadcasted_iota(jnp.int32, (n_rows, slots), 1) == target_col, 1.0, 0.0
    ).astype(bf16)
    rw = jnp.sum(jnp.where(eye, rw_ref[...], 0.0), axis=1, keepdims=True)
    for part, columns in ((1, slice(wa, width)), (0, slice(0, wa))):

        @pl.loop(1, groups)
        def _(k):
            d = lax.rem(g + k, groups)
            arrived(ret_in[part].at[d], ret_s.at[part, d], ret_r.at[part, d])

        returned = jnp.concatenate([ret_in[part][d] for d in range(groups)], axis=0)
        combined = jnp.dot(places_t, returned, preferred_element_type=f32)
        o_ref[:, columns] = (combined * rw).astype(o_ref.dtype)


def body(pair_rows, group_ids, local_ids, route_weight, w_up, w_down):
    groups = lax.axis_size("group")
    n_rows, width = pair_rows.shape
    cap = 2 * n_rows // groups
    slots = groups * cap
    wa = 8 * width // 16
    wb = width - wa
    wide = width + TAG
    dma = pltpu.SemaphoreType.DMA
    vmem, hbm = pl.BlockSpec(memory_space=pltpu.VMEM), pl.BlockSpec(memory_space=pl.ANY)
    V = pltpu.VMEM
    scratch = [
        V((n_rows, width), bf16), V((1, n_rows), jnp.int32), V((1, n_rows), jnp.int32), V((1, n_rows), f32), dma((4,)),
        V(w_up.shape, bf16), V(w_down.shape, bf16), dma((2,)),
        V((groups, cap, wide), bf16), V((groups, cap, wide), bf16), dma((groups,)), dma((groups,)),
        V((ZS, XS, slots, wa), bf16), V((ZS, XS, slots, wb + TAG), bf16),
        dma((XS,)), dma((XS,)), dma((2, 4, XS)), dma((2, 4, XS)), dma((2, 4)), dma((2, 4)), dma((XS, ZS)), dma((XS, ZS)),
        V((ZS, XS, slots, wa), bf16), V((ZS, XS, slots, wb), bf16),
        dma((2, 4, XS)), dma((2, 4, XS)), V((2, 4, XS, slots, wa), bf16), dma((XS,)), dma((XS,)),
        V((XS, slots, wa), bf16), V((XS, slots, wa), bf16),
        dma((3, ZS)), dma((3, ZS)), V((3, ZS, slots, wb), bf16), V((ZS, slots, wb), bf16),
        dma((2, 4)), dma((2, 4)), V((2, 4, slots, wb), bf16), V((2, 4, slots, wb), bf16),
        [V((groups, cap, w), bf16) for w in (wa, wb)], [V((groups, cap, w), bf16) for w in (wa, wb)],
        dma((2, groups)), dma((2, groups)),
    ]
    return pl.pallas_call(
        kernel,
        out_shape=jax.ShapeDtypeStruct((n_rows, width), bf16),
        in_specs=[hbm] * 6,
        out_specs=vmem,
        scratch_shapes=scratch,
        compiler_params=pltpu.CompilerParams(
            collective_id=0, has_side_effects=True, vmem_limit_bytes=56 * 2**20
        ),
        name="routed_experts",
    )(
        pair_rows,
        group_ids.reshape(1, n_rows),
        local_ids.reshape(1, n_rows),
        route_weight.reshape(1, n_rows),
        w_up,
        w_down,
    )


def solution(mesh):
    placed = (
        P(("group", "inner"), None),
        P(("group", "inner"), None),
        P(("group", "inner"), None),
        P(("group", "inner")),
        P("group", None, "inner"),
        P("group", "inner", None),
    )
    return jax.shard_map(
        body, mesh=mesh, in_specs=placed, out_specs=P(("group", "inner"), None), check_vma=False
    )
```
